128 devices in a mesh: span: 8 (over z, y_hi), chord: 16 (over y_lo, x, core).
Axes of the slice: x: 4, y: 4 (y_hi: 2, y_lo: 2; y = y_hi * 2 + y_lo), z: 4, core: 2. Of those that a mesh axis runs over, the one named last changes fastest.
Arguments:
- adjoint_next: float32 [5, 128, 512, 256], P(None, 'span', 'chord'), may hold values from -6 to 6
- objective_grad: bfloat16 [5, 128, 512, 256], P(None, 'span', 'chord'), may hold values from -6 to 6
- state_next: bfloat16 [8, 128, 512, 256], P(None, 'span', 'chord'), may hold values from -3 to 3, as said below
- checkpoint_pieces: bfloat16 [8, 16384, 1024], P(None, ('span', 'chord')), may hold values from -3 to 3, as said below
- slot_target: int32 [128, 128], P(('span', 'chord')), may hold values from 0 to 127, as said below
- piece_owner: int32 [128, 128], P(('span', 'chord')), may hold values from 0 to 127, as said below
- coupling: float32 [5, 5], replicated, may hold values from -1.5 to 1.5
Outputs:
- adjoint_field: float32 [5, 128, 512, 256], P(None, 'span', 'chord')
The draws below stay inside these ranges and needn't reach their ends.
Inputs may be any that keep to these rules, and one draw needn't show every extreme that they name: `state_next`: fields 0 and 4 (density, energy) lie in [0.5, 2], fields 5 to 7 in [-1.5, 1.5]. `checkpoint_pieces`: fields 0 and 4 (density, energy) lie in [0.5, 2], fields 5 to 7 in [-1.5, 1.5]. `slot_target`: each row lists every device index once: an owner holds exactly one piece of every device's block. `piece_owner`: each row lists every owner once.
All inputs are finite; a program needn't handle non-finite values.
Results may differ from the reference program's by a relative error of at most 0.0003.
Values may be sent and summed in bfloat16 or wider, within the bound.
No kernel may reach another device: no remote copies, remote signals or barrier semaphores. Data moves between devices by JAX's collectives and lax.ppermute only.
A program may use at most 256 MiB of HBM per device.

```python
import jax
import jax.numpy as jnp
from jax import lax

NCONS = 5
NSTATE = 8
CS = 16
CC = 32
CN = 256
SWEEPS = 4
BLOCKS = 128
PIECE = 1024
NS = 128
NC = 512
N_SPAN = 8
N_CHORD = 16


def state_law(key, extent):
    density_key, flow_key = jax.random.split(key)
    uniform_part = jax.random.uniform(density_key, extent, jnp.float32)
    flow_draw = jnp.clip(jax.random.normal(flow_key, extent, jnp.float32), -3.0, 3.0)
    field_index = lax.broadcasted_iota(jnp.int32, extent, 0)
    positive = 0.5 + 1.5 * uniform_part
    moving = jnp.where(field_index >= 5, 0.5 * flow_draw, flow_draw)
    return jnp.where((field_index == 0) | (field_index == 4), positive, moving)


def draw_state_next(key, part):
    return state_law(jax.random.fold_in(key, 11), (NSTATE, NS, NC, CN)).astype(jnp.bfloat16)


def draw_checkpoint_pieces(key, part):
    return state_law(jax.random.fold_in(key, 12), (NSTATE, BLOCKS * BLOCKS, PIECE)).astype(jnp.bfloat16)


def permuted_rows(key):
    row_keys = jax.random.split(key, BLOCKS)

    def one_row(row_key):
        return jax.random.permutation(row_key, BLOCKS).astype(jnp.int32)
    return jax.vmap(one_row)(row_keys)


def draw_slot_target(key, part):
    return permuted_rows(jax.random.fold_in(key, 21))


def draw_piece_owner(key, part):
    return permuted_rows(jax.random.fold_in(key, 22))


def shard_levels(key, shape, cuts, smallest, high):
    def one(position, shards_of):
        steps = jax.random.uniform(jax.random.fold_in(jax.random.fold_in(key, 6), position), (shards_of,), jnp.float32, smallest / len(cuts), high / len(cuts))
        return jnp.repeat(jnp.exp(steps), shape[position] // shards_of).reshape((-1,) + (1,) * (len(shape) - position - 1))

    level = one(*cuts[0])
    for cut in cuts[1:]:
        level = level * one(*cut)
    return level


def bell_draw(key, shape, width, reach, cuts=(), held_as=jnp.bfloat16):
    entries = width * jax.random.normal(key, shape, jnp.float32)
    if cuts:
        entries = entries * shard_levels(key, shape, cuts, -0.22, 0.18)
    return jnp.clip(entries, -reach, reach).astype(held_as)


def setup_inputs(seed: int = 0) -> dict:
    key_of = jax.random.split(jax.random.key(seed), 8)
    adjoint_next = bell_draw(key_of[0], (NCONS, NS, NC, CN), 1.0, 6.0, ((1, 8), (2, 16)), jnp.float32)
    objective_grad = bell_draw(key_of[1], (NCONS, NS, NC, CN), 1.0, 6.0, ((1, 8), (2, 16)))
    state_next = draw_state_next(jax.random.fold_in(key_of[7], 71), 0)
    checkpoint_pieces = draw_checkpoint_pieces(jax.random.fold_in(key_of[7], 71), 0)
    slot_target = draw_slot_target(jax.random.fold_in(key_of[7], 71), 0)
    piece_owner = draw_piece_owner(jax.random.fold_in(key_of[7], 71), 0)
    coupling = bell_draw(key_of[6], (NCONS, NCONS), 0.3, 1.5, (), jnp.float32)
    return {"adjoint_next": adjoint_next, "objective_grad": objective_grad, "state_next": state_next, "checkpoint_pieces": checkpoint_pieces, "slot_target": slot_target, "piece_owner": piece_owner, "coupling": coupling}


inverse_step = 1.0
dissipation_floor = 0.25


def coefficients(state):
    fields = state.astype(jnp.float32)
    density = fields[0]
    velocity = fields[1:4] / density - fields[5:8]
    viscosity = 0.5 * jnp.abs(velocity) + dissipation_floor
    energy_ratio = fields[4] / density
    return velocity, viscosity, energy_ratio


def combine(adjoint, uppers, lowers, coefficient_set, coupling):
    velocity, viscosity, energy_ratio = coefficient_set
    operated_sum = jnp.einsum("nm,nxyz->mxyz", coupling, adjoint, precision=lax.Precision.HIGHEST) * energy_ratio
    for direction in range(3):
        upper_cells = uppers[direction]
        lower_cells = lowers[direction]
        operated_sum = operated_sum + 0.5 * velocity[direction] * (upper_cells - lower_cells) + viscosity[direction] * (2.0 * adjoint - upper_cells - lower_cells)
    return operated_sum


def shifted(adjoint):
    padded = jnp.pad(adjoint, ((0, 0), (1, 1), (1, 1), (1, 1)))
    uppers = (padded[:, 2:, 1:-1, 1:-1], padded[:, 1:-1, 2:, 1:-1], padded[:, 1:-1, 1:-1, 2:])
    lowers = (padded[:, :-2, 1:-1, 1:-1], padded[:, 1:-1, :-2, 1:-1], padded[:, 1:-1, 1:-1, :-2])
    return uppers, lowers


def assemble(checkpoint_pieces, slot_target, piece_owner):
    owners = jnp.arange(BLOCKS, dtype=jnp.int32)
    columns = jnp.broadcast_to(owners[None, :], (BLOCKS, BLOCKS))
    slot_lookup = jnp.zeros((BLOCKS, BLOCKS), jnp.int32).at[owners[:, None], slot_target].set(columns)
    targets = jnp.broadcast_to(owners[:, None], (BLOCKS, BLOCKS))
    slots = piece_owner * BLOCKS + slot_lookup[piece_owner, targets]
    chosen = jnp.take(checkpoint_pieces, slots.reshape(-1).astype(jnp.int32), axis=1)
    blocks = chosen.reshape(NSTATE, N_SPAN, N_CHORD, CS, CC, CN).transpose(0, 1, 3, 2, 4, 5)
    return blocks.reshape(NSTATE, NS, NC, CN).astype(jnp.float32)


def reference(adjoint_next, objective_grad, state_next, checkpoint_pieces, slot_target, piece_owner, coupling):
    next_set = coefficients(state_next)
    uppers, lowers = shifted(adjoint_next)
    right_side = adjoint_next * inverse_step - 0.5 * combine(adjoint_next, uppers, lowers, next_set, coupling) + objective_grad.astype(jnp.float32)
    state_now = assemble(checkpoint_pieces, slot_target, piece_owner)
    now_set = coefficients(state_now)
    viscosity_sum = jnp.sum(now_set[1], axis=0)
    diagonal = inverse_step + viscosity_sum
    adjoint = adjoint_next
    for repeat in range(SWEEPS):
        uppers, lowers = shifted(adjoint)
        operated = combine(adjoint, uppers, lowers, now_set, coupling)
        adjoint = (right_side - 0.5 * (operated - 2.0 * viscosity_sum * adjoint)) / diagonal
    return adjoint
```

```python
import functools

import jax
import jax.numpy as jnp
from jax import lax
from jax.experimental import pallas as pl
from jax.experimental.pallas import tpu as pltpu
from jax.sharding import PartitionSpec as P

NCONS = 5
NSTATE = 8
CS = 16
CC = 32
CN = 256
SWEEPS = 4
PIECE = 1024
TILES = CC // 8
LANES = 128
HALVES = CN // LANES
VELOCITY_CODE = 4368.0
ENERGY_CODE = 8190.0
MIB = 1 << 20


def in_vmem(array):
    return pltpu.with_memory_space_constraint(array, pltpu.VMEM)


def call(body, outs, args, scratch=(), name=None, smem=(), limit=24 * MIB, cost=4000000):
    specs = [
        pl.BlockSpec(memory_space=pltpu.SMEM if i in smem else pltpu.VMEM) for i in range(len(args))
    ]
    return pl.pallas_call(
        body,
        out_shape=[pltpu.VMEM(shape, dtype) for shape, dtype in outs],
        in_specs=specs,
        out_specs=[pl.BlockSpec(memory_space=pltpu.VMEM) for _ in outs],
        scratch_shapes=list(scratch),
        compiler_params=pltpu.CompilerParams(vmem_limit_bytes=limit),
        cost_estimate=pl.CostEstimate(flops=cost * 8, bytes_accessed=cost, transcendentals=0),
        name=name,
    )(*[a if i in smem else in_vmem(a) for i, a in enumerate(args)])


def lanes(half):
    return pl.ds(half * LANES, LANES)


def rows(tile):
    return pl.ds(tile * 8, 8)


def mask_of(shape_dim, value):
    return lax.broadcasted_iota(jnp.int32, (8, LANES), shape_dim) == value


class Field:
    def __init__(self, cells, span_low, span_high, chord_low, chord_high):
        self.cells = cells
        self.span_low = span_low
        self.span_high = span_high
        self.chord_low = chord_low
        self.chord_high = chord_high

    def center(self, m, s, t, h):
        return self.cells[m, s, rows(t), lanes(h)]

    def span(self, m, s, t, h, step, edge):
        if edge == step:
            source = self.span_high if step > 0 else self.span_low
            return source[m, rows(t), lanes(h)]
        return self.cells[m, s + step, rows(t), lanes(h)]

    def chord(self, m, s, t, h, step, center, first, last):
        if step > 0:
            if t == TILES - 1:
                beyond = jnp.broadcast_to(self.chord_high[s, pl.ds(m, 1), lanes(h)], (8, LANES))
            else:
                beyond = self.center(m, s, t + 1, h)
            return pltpu.roll(jnp.where(first, beyond, center), 7, 0)
        if t == 0:
            beyond = jnp.broadcast_to(self.chord_low[s, pl.ds(m, 1), lanes(h)], (8, LANES))
        else:
            beyond = self.center(m, s, t - 1, h)
        return pltpu.roll(jnp.where(last, beyond, center), 1, 0)


def normal(centers, h, step, lane_first, lane_last):
    if step > 0:
        source = jnp.where(lane_first, centers[h + 1], centers[h]) if h + 1 < HALVES else centers[h]
        return pltpu.roll(source, LANES - 1, 1)
    source = jnp.where(lane_last, centers[h - 1], centers[h]) if h > 0 else centers[h]
    return pltpu.roll(source, 1, 1)


def stencil(field, s, t, edge, factors, energies, bases, coupling):
    row_first, row_last = mask_of(0, 0), mask_of(0, 7)
    lane_first, lane_last = mask_of(1, 0), mask_of(1, LANES - 1)
    centers = [[field.center(m, s, t, h) for h in range(HALVES)] for m in range(NCONS)]
    out = []
    for m in range(NCONS):
        scalars = [coupling[n, m] for n in range(NCONS)]
        pair = []
        for h in range(HALVES):
            (span_up, span_low), (chord_up, chord_low), (normal_up, normal_low) = factors[h]
            mixed = scalars[0] * centers[0][h]
            for n in range(1, NCONS):
                mixed = mixed + scalars[n] * centers[n][h]
            total = bases(m, h, centers[m][h]) + energies[h] * mixed
            total = total + span_up * field.span(m, s, t, h, 1, edge)
            total = total + span_low * field.span(m, s, t, h, -1, edge)
            total = total + chord_up * field.chord(m, s, t, h, 1, centers[m][h], row_first, row_last)
            total = total + chord_low * field.chord(m, s, t, h, -1, centers[m][h], row_first, row_last)
            total = total + normal_up * normal(centers[m], h, 1, lane_first, lane_last)
            total = total + normal_low * normal(centers[m], h, -1, lane_first, lane_last)
            pair.append(total)
        out.append(pair)
    return out


def each_row(row):
    row(0, -1)

    def inner(s, carry):
        row(s, 0)
        return carry

    lax.fori_loop(1, CS - 1, inner, 0)
    row(CS - 1, 1)


def halves_of(velocity, h):
    pairs = []
    for a in range(3):
        up = jnp.maximum(-velocity[a], 0.0) + 0.25
        low = jnp.maximum(velocity[a], 0.0) + 0.25
        if a == 2 and h == HALVES - 1:
            up = jnp.where(mask_of(1, LANES - 1), 0.0, up)
        if a == 2 and h == 0:
            low = jnp.where(mask_of(1, 0), 0.0, low)
        pairs.append((up, low))
    return pairs


def write_edges(out, s, t, edge, span_low, span_high, chord_low, chord_high):
    for m in range(NCONS):
        for h in range(HALVES):
            tile = out[m][h]
            if edge == -1:
                span_low[m, rows(t), lanes(h)] = tile
            if edge == 1:
                span_high[m, rows(t), lanes(h)] = tile
            if t == 0:
                chord_low[s, pl.ds(m, 1), lanes(h)] = tile[0:1]
            if t == TILES - 1:
                chord_high[s, pl.ds(m, 1), lanes(h)] = tile[7:8]


def send_body(pieces, target, out, words):
    groups = pieces.shape[1] // 16

    def group(g, carry):
        for c in range(PIECE // LANES):
            read = lambda f: pieces[f, pl.ds(g * 16, 16), lanes(c)].astype(jnp.float32)
            ratio = 1.0 / read(0)
            codes = [jnp.round((read(1 + a) * ratio - read(5 + a)) * VELOCITY_CODE).astype(jnp.int32) for a in range(3)]
            codes.append(jnp.round(read(4) * ratio * ENERGY_CODE).astype(jnp.int32))
            for w in range(2):
                word = (codes[2 * w] << 16) | (codes[2 * w + 1] & 0xFFFF)
                for part in range(2):
                    words[w, pl.ds((g * 2 + part) * 64 + c * 8, 8), :] = word[part * 8 : part * 8 + 8]
        for j in range(16):
            d = target[0, g * 16 + j]
            for w in range(2):
                out[d, pl.ds(w * 8, 8), :] = words[w, pl.ds((g * 2 + j // 8) * 64 + j % 8, 8, stride=8), :]
        return carry

    lax.fori_loop(0, groups, group, 0)


def send_order(pieces, target):
    count = pieces.shape[1]
    return call(
        send_body,
        [((count, 16, LANES), jnp.int32)],
        [pieces, target],
        scratch=[pltpu.VMEM((2, count * 8, LANES), jnp.int32)],
        smem=(1,),
        name="send_order",
        cost=3 * MIB,
    )[0]


def right_body(v, state, grad, coupling, sl, sh, cl, ch, out):
    field = Field(v, sl, sh, cl, ch)

    def row(s, edge):
        for pair in range(TILES // 2):
            wide = lambda ref, f, h: ref[f, s, pl.ds(pair * 16, 16), lanes(h)].astype(jnp.float32)
            fields = [[wide(state, f, h) for h in range(HALVES)] for f in range(NSTATE)]
            gradient = [[wide(grad, m, h) for h in range(HALVES)] for m in range(NCONS)]
            for part in range(2):
                t = pair * 2 + part
                cut = lambda x: x[part * 8 : part * 8 + 8]
                factors, energies, middles = [], [], []
                for h in range(HALVES):
                    ratio = 1.0 / cut(fields[0][h])
                    velocity = [cut(fields[1 + a][h]) * ratio - cut(fields[5 + a][h]) for a in range(3)]
                    factors.append([(0.5 * up, 0.5 * low) for up, low in halves_of(velocity, h)])
                    energies.append(-0.5 * (cut(fields[4][h]) * ratio))
                    size = jnp.abs(velocity[0]) + jnp.abs(velocity[1]) + jnp.abs(velocity[2])
                    middles.append(0.25 - 0.5 * size)
                base = lambda m, h, center: cut(gradient[m][h]) + middles[h] * center
                result = stencil(field, s, t, edge, factors, energies, base, coupling)
                for m in range(NCONS):
                    for h in range(HALVES):
                        out[m, s, rows(t), lanes(h)] = result[m][h]

    each_row(row)


def first_body(v, words, owner, right, coupling, sl, sh, cl, ch, out, factor, scaled, el, eh, fl, fh, placed):
    field = Field(v, sl, sh, cl, ch)

    def place(k, carry):
        o = owner[0, k]
        for w in range(2):
            placed[w, pl.ds(pl.multiple_of(k * 8, 8), 8), :] = words[o, pl.ds(w * 8, 8), :]
        return carry

    lax.fori_loop(0, owner.shape[1], place, 0, unroll=8)

    def row(s, edge):
        for t in range(TILES):
            factors, energies, scales = [], [], []
            for h in range(HALVES):
                pair = [placed[w, pl.ds((s * 8 + t * 2) * 8 + h, 8, stride=2), :] for w in range(2)]
                codes = []
                for word in pair:
                    codes += [(word >> 16).astype(jnp.float32), ((word << 16) >> 16).astype(jnp.float32)]
                velocity = [codes[a] * (1.0 / VELOCITY_CODE) for a in range(3)]
                size = jnp.abs(velocity[0]) + jnp.abs(velocity[1]) + jnp.abs(velocity[2])
                scale = 1.0 / (1.75 + 0.5 * size)
                half = 0.5 * scale
                pairs = [(half * up, half * low) for up, low in halves_of(velocity, h)]
                energy = (-1.0 / ENERGY_CODE) * codes[3] * half
                factors.append(pairs)
                energies.append(energy)
                scales.append(scale)
                for a in range(3):
                    factor[2 * a, s, rows(t), lanes(h)] = pairs[a][0]
                    factor[2 * a + 1, s, rows(t), lanes(h)] = pairs[a][1]
                factor[6, s, rows(t), lanes(h)] = energy

            def base(m, h, center):
                value = right[m, s, rows(t), lanes(h)] * scales[h]
                scaled[m, s, rows(t), lanes(h)] = value
                return value

            result = stencil(field, s, t, edge, factors, energies, base, coupling)
            for m in range(NCONS):
                for h in range(HALVES):
                    out[m, s, rows(t), lanes(h)] = result[m][h]
            write_edges(result, s, t, edge, el, eh, fl, fh)

    each_row(row)


def sweep_body(edges, v, factor, scaled, coupling, sl, sh, cl, ch, out, *faces):
    field = Field(v, sl, sh, cl, ch)

    def row(s, edge):
        for t in range(TILES):
            read = lambda i, h: factor[i, s, rows(t), lanes(h)]
            factors = [[(read(2 * a, h), read(2 * a + 1, h)) for a in range(3)] for h in range(HALVES)]
            energies = [read(6, h) for h in range(HALVES)]
            base = lambda m, h, center: scaled[m, s, rows(t), lanes(h)]
            result = stencil(field, s, t, edge, factors, energies, base, coupling)
            for m in range(NCONS):
                for h in range(HALVES):
                    out[m, s, rows(t), lanes(h)] = result[m][h]
            if edges:
                write_edges(result, s, t, edge, *faces)

    each_row(row)


CELLS = ((NCONS, CS, CC, CN), jnp.float32)
FACES = [((NCONS, CC, CN), jnp.float32)] * 2 + [((CS, NCONS, CN), jnp.float32)] * 2


def exchange(faces):
    span_low, span_high, chord_low, chord_high = faces
    move = lambda x, axis, up: lax.ppermute(
        x,
        axis,
        [(i, i + 1) if up else (i + 1, i) for i in range(lax.axis_size(axis) - 1)],
    )
    return (
        move(span_high, "span", True),
        move(span_low, "span", False),
        move(chord_high, "chord", True),
        move(chord_low, "chord", False),
    )


def shards(adjoint_next, objective_grad, state_next, checkpoint_pieces, slot_target, piece_owner, coupling):
    outgoing = send_order(checkpoint_pieces, slot_target)
    incoming = lax.all_to_all(outgoing, ("span", "chord"), split_axis=0, concat_axis=0, tiled=True)
    halo = exchange(
        (
            adjoint_next[:, 0],
            adjoint_next[:, CS - 1],
            adjoint_next[:, :, 0].transpose(1, 0, 2),
            adjoint_next[:, :, CC - 1].transpose(1, 0, 2),
        )
    )
    right = call(
        right_body,
        [CELLS],
        [adjoint_next, state_next, objective_grad, coupling, *halo],
        smem=(3,),
        name="right_side",
        cost=9 * MIB,
    )[0]
    adjoint, factor, scaled, *faces = call(
        first_body,
        [CELLS, ((7, CS, CC, CN), jnp.float32), CELLS, *FACES],
        [adjoint_next, incoming, piece_owner, right, coupling, *halo],
        scratch=[pltpu.VMEM((2, 1024, LANES), jnp.int32)],
        smem=(2, 4),
        name="first_sweep",
        cost=9 * MIB,
    )
    for sweep in range(1, SWEEPS):
        more = sweep < SWEEPS - 1
        adjoint, *faces = call(
            functools.partial(sweep_body, more),
            [CELLS, *(FACES if more else [])],
            [adjoint, factor, scaled, coupling, *exchange(faces)],
            smem=(3,),
            name="sweep",
            cost=9 * MIB,
        )
    return adjoint


def solution(mesh):
    placed = (
        P(None, "span", "chord", None),
        P(None, "span", "chord", None),
        P(None, "span", "chord", None),
        P(None, ("span", "chord"), None),
        P(("span", "chord"), None),
        P(("span", "chord"), None),
        P(),
    )
    return jax.shard_map(
        shards,
        mesh=mesh,
        in_specs=placed,
        out_specs=P(None, "span", "chord", None),
        check_vma=False,
    )
```

```python
import jax
import jax.numpy as jnp
from jax import lax
from jax.experimental import pallas as pl
from jax.experimental.pallas import tpu as pltpu
from jax.sharding import PartitionSpec as P

NCONS = 5
NSTATE = 8
CS = 16
CC = 32
CN = 256
SWEEPS = 4
PIECE = 1024
TILES = CC // 8
LANES = 128
HALVES = CN // LANES
VELOCITY_CODE = 4368.0
ENERGY_CODE = 8190.0
MIB = 1 << 20
F32 = jnp.float32
BF16 = jnp.bfloat16


def in_space(array, space):
    return pltpu.with_memory_space_constraint(array, space)


def call(body, outs, args, scratch=(), name=None, smem=(), hbm=(), hbm_outs=(), limit=24 * MIB, cost=4 * MIB):
    space = lambda i: pltpu.SMEM if i in smem else pltpu.HBM if i in hbm else pltpu.VMEM
    out_space = lambda i: pltpu.HBM if i in hbm_outs else pltpu.VMEM
    return pl.pallas_call(
        body,
        out_shape=[out_space(i)(shape, dtype) for i, (shape, dtype) in enumerate(outs)],
        in_specs=[pl.BlockSpec(memory_space=space(i)) for i in range(len(args))],
        out_specs=[pl.BlockSpec(memory_space=out_space(i)) for i in range(len(outs))],
        scratch_shapes=list(scratch),
        compiler_params=pltpu.CompilerParams(vmem_limit_bytes=limit),
        cost_estimate=pl.CostEstimate(flops=cost * 8, bytes_accessed=cost, transcendentals=0),
        name=name,
    )(*[a if i in smem else in_space(a, space(i)) for i, a in enumerate(args)])


def lanes(half):
    return pl.ds(half * LANES, LANES)


def rows(tile):
    return pl.ds(tile * 8, 8)


def wide_rows(pair):
    return pl.ds(pair * 16, 16)


def mask_of(dim, value):
    return lax.broadcasted_iota(jnp.int32, (8, LANES), dim) == value


SPAN_FACE = ((NCONS, CC, CN), BF16)
CHORD_FACE = ((CS // 2, 16, CN), BF16)
FACES = [SPAN_FACE, SPAN_FACE, CHORD_FACE, CHORD_FACE]
SPAN_HALO = pltpu.VMEM((2, NCONS, CC, CN), F32)
CHORD_HALO = pltpu.VMEM((2, CS, 8, CN), F32)


def parity(axis):
    return lax.rem(lax.axis_index(axis), 2)


def unpack_faces(faces, span_halo, chord_halo):
    span_a, span_b, chord_a, chord_b = faces
    p = parity("span")
    for face, side in ((span_a, 1 - p), (span_b, p)):
        for m in range(NCONS):
            for pair in range(CC // 16):
                span_halo[side, m, wide_rows(pair), :] = face[m, wide_rows(pair), :].astype(F32)
    p = parity("chord")
    for face, side in ((chord_a, 1 - p), (chord_b, p)):
        for group in range(CS // 2):
            both = face[group].astype(F32)
            chord_halo[side, 2 * group] = both[:8]
            chord_halo[side, 2 * group + 1] = both[8:]


def pack_faces(cells, chord_edge, faces):
    span_a, span_b, chord_a, chord_b = faces
    p = parity("span")
    for face, side in ((span_a, 1 - p), (span_b, p)):
        for m in range(NCONS):
            for pair in range(CC // 16):
                face[m, wide_rows(pair), :] = cells[m, side * (CS - 1), wide_rows(pair), :].astype(BF16)
    p = parity("chord")
    for face, side in ((chord_a, 1 - p), (chord_b, p)):
        for group in range(CS // 2):
            both = [chord_edge[side, 2 * group], chord_edge[side, 2 * group + 1]]
            face[group] = jnp.concatenate(both, axis=0).astype(BF16)


def clear_padding(chord_edge):
    for side in range(2):
        for s in range(CS):
            chord_edge[side, s] = jnp.zeros((8, CN), F32)


def faces_body(cells, span_a, span_b, chord_a, chord_b, chord_edge):
    clear_padding(chord_edge)
    for s in range(CS):
        for m in range(NCONS):
            chord_edge[0, s, pl.ds(m, 1), :] = cells[m, s, pl.ds(0, 1), :]
            chord_edge[1, s, pl.ds(m, 1), :] = cells[m, s, pl.ds(CC - 1, 1), :]
    pack_faces(cells, chord_edge, (span_a, span_b, chord_a, chord_b))


def exchange(faces):
    def swap(face, axis, start):
        count = lax.axis_size(axis)
        pairs = [(i, i + 1) for i in range(start, count - 1, 2)]
        return lax.ppermute(face, axis, pairs + [(b, a) for a, b in pairs])

    span_a, span_b, chord_a, chord_b = faces
    return swap(span_a, "span", 0), swap(span_b, "span", 1), swap(chord_a, "chord", 0), swap(chord_b, "chord", 1)


class Field:
    def __init__(self, cells, span_halo, chord_halo):
        self.cells = cells
        self.span_halo = span_halo
        self.chord_halo = chord_halo

    def center(self, m, s, t, h):
        return self.cells[m, s, rows(t), lanes(h)]

    def span(self, m, s, t, h, step, edge):
        if edge == step:
            return self.span_halo[1 if step > 0 else 0, m, rows(t), lanes(h)]
        return self.cells[m, s + step, rows(t), lanes(h)]

    def beyond(self, side, m, s, h):
        return jnp.broadcast_to(self.chord_halo[side, s, pl.ds(m, 1), lanes(h)], (8, LANES))

    def chord(self, m, s, t, h, step, center, first, last):
        if step > 0:
            after = self.beyond(1, m, s, h) if t == TILES - 1 else self.center(m, s, t + 1, h)
            return pltpu.roll(jnp.where(first, after, center), 7, 0)
        before = self.beyond(0, m, s, h) if t == 0 else self.center(m, s, t - 1, h)
        return pltpu.roll(jnp.where(last, before, center), 1, 0)


def normal(centers, h, step, lane_first, lane_last):
    if step > 0:
        source = jnp.where(lane_first, centers[h + 1], centers[h]) if h + 1 < HALVES else centers[h]
        return pltpu.roll(source, LANES - 1, 1)
    source = jnp.where(lane_last, centers[h - 1], centers[h]) if h > 0 else centers[h]
    return pltpu.roll(source, 1, 1)


def stencil(field, s, t, edge, factors, energies, bases, coupling):
    row_first, row_last = mask_of(0, 0), mask_of(0, 7)
    lane_first, lane_last = mask_of(1, 0), mask_of(1, LANES - 1)
    centers = [[field.center(m, s, t, h) for h in range(HALVES)] for m in range(NCONS)]
    out = []
    for m in range(NCONS):
        scalars = [coupling[n, m] for n in range(NCONS)]
        pair = []
        for h in range(HALVES):
            (span_up, span_low), (chord_up, chord_low), (normal_up, normal_low) = factors[h]
            mixed = scalars[0] * centers[0][h]
            for n in range(1, NCONS):
                mixed = mixed + scalars[n] * centers[n][h]
            total = bases(m, h, centers[m][h]) + energies[h] * mixed
            total = total + span_up * field.span(m, s, t, h, 1, edge)
            total = total + span_low * field.span(m, s, t, h, -1, edge)
            total = total + chord_up * field.chord(m, s, t, h, 1, centers[m][h], row_first, row_last)
            total = total + chord_low * field.chord(m, s, t, h, -1, centers[m][h], row_first, row_last)
            total = total + normal_up * normal(centers[m], h, 1, lane_first, lane_last)
            total = total + normal_low * normal(centers[m], h, -1, lane_first, lane_last)
            pair.append(total)
        out.append(pair)
    return out


def each_row(row):
    row(0, -1)

    def inner(s, carry):
        row(s, 0)
        return carry

    lax.fori_loop(1, CS - 1, inner, 0)
    row(CS - 1, 1)


def halves_of(velocity, h):
    pairs = []
    for a in range(3):
        up = jnp.maximum(-velocity[a], 0.0) + 0.25
        low = jnp.maximum(velocity[a], 0.0) + 0.25
        if a == 2 and h == HALVES - 1:
            up = jnp.where(mask_of(1, LANES - 1), 0.0, up)
        if a == 2 and h == 0:
            low = jnp.where(mask_of(1, 0), 0.0, low)
        pairs.append((up, low))
    return pairs


def put(out, result, s, t, chord_edge=None):
    for m in range(NCONS):
        for h in range(HALVES):
            tile = result[m][h]
            out[m, s, rows(t), lanes(h)] = tile
            if chord_edge is not None and t == 0:
                chord_edge[0, s, pl.ds(m, 1), lanes(h)] = tile[0:1]
            if chord_edge is not None and t == TILES - 1:
                chord_edge[1, s, pl.ds(m, 1), lanes(h)] = tile[7:8]


SLOTS = 16


def send_body(pieces, target, out, taken, words, ordered, in_sem, out_sem):
    groups = pieces.shape[1] // SLOTS
    take = lambda g: pltpu.make_async_copy(
        pieces.at[:, pl.ds(g * SLOTS, SLOTS)], taken.at[:, pl.ds(g * SLOTS, SLOTS)], in_sem.at[g]
    )
    for g in range(groups):
        take(g).start()

    def group(g, carry):
        take(g).wait()
        for c in range(PIECE // LANES):
            read = lambda f: taken[f, pl.ds(pl.multiple_of(g * SLOTS, SLOTS), SLOTS), lanes(c)].astype(F32)
            ratio = 1.0 / read(0)
            codes = [jnp.round((read(1 + a) * ratio - read(5 + a)) * VELOCITY_CODE).astype(jnp.int32) for a in range(3)]
            codes.append(jnp.round(read(4) * ratio * ENERGY_CODE).astype(jnp.int32))
            for w in range(2):
                word = (codes[2 * w] << 16) | (codes[2 * w + 1] & 0xFFFF)
                for part in range(2):
                    at = pl.multiple_of((g * 2 + part) * 64 + c * 8, 8)
                    words[w, pl.ds(at, 8), :] = word[part * 8 : part * 8 + 8]
        for j in range(SLOTS):
            d = target[0, g * SLOTS + j]
            for w in range(2):
                ordered[d, w] = words[w, pl.ds((g * 2 + j // 8) * 64 + j % 8, 8, stride=8), :]
        return carry

    lax.fori_loop(0, groups, group, 0)
    copy = pltpu.make_async_copy(ordered, out, out_sem)
    copy.start()
    copy.wait()


def send_order(pieces, target):
    count = pieces.shape[1]
    return call(
        send_body,
        [((count, 2, 8, LANES), jnp.int32)],
        [pieces, target],
        scratch=[
            pltpu.VMEM(pieces.shape, BF16),
            pltpu.VMEM((2, count * 8, LANES), jnp.int32),
            pltpu.VMEM((count, 2, 8, LANES), jnp.int32),
            pltpu.SemaphoreType.DMA((count // SLOTS,)),
            pltpu.SemaphoreType.DMA,
        ],
        smem=(1,),
        hbm=(0,),
        hbm_outs=(0,),
        name="send_order",
        cost=3 * MIB,
    )[0]


def right_body(v, state, grad, coupling, fa, fb, fc, fd, out, states, grads, rights, span_halo, chord_halo, in_sem, out_sem):
    copies = lambda s: (
        pltpu.make_async_copy(state.at[:, s], states.at[:, s], in_sem.at[0, s]),
        pltpu.make_async_copy(grad.at[:, s], grads.at[:, s], in_sem.at[1, s]),
    )
    put_out = lambda s: pltpu.make_async_copy(rights.at[:, s], out.at[:, s], out_sem.at[s])
    for s in range(CS):
        for copy in copies(s):
            copy.start()
    unpack_faces((fa, fb, fc, fd), span_halo, chord_halo)
    field = Field(v, span_halo, chord_halo)

    def row(s, edge):
        for copy in copies(s):
            copy.wait()
        for pair in range(TILES // 2):
            wide = lambda ref, f, h: ref[f, s, wide_rows(pair), lanes(h)].astype(F32)
            fields = [[wide(states, f, h) for h in range(HALVES)] for f in range(NSTATE)]
            gradient = [[wide(grads, m, h) for h in range(HALVES)] for m in range(NCONS)]
            for part in range(2):
                t = pair * 2 + part
                cut = lambda x: x[part * 8 : part * 8 + 8]
                factors, energies, middles = [], [], []
                for h in range(HALVES):
                    ratio = 1.0 / cut(fields[0][h])
                    velocity = [cut(fields[1 + a][h]) * ratio - cut(fields[5 + a][h]) for a in range(3)]
                    factors.append([(0.5 * up, 0.5 * low) for up, low in halves_of(velocity, h)])
                    energies.append(-0.5 * (cut(fields[4][h]) * ratio))
                    size = jnp.abs(velocity[0]) + jnp.abs(velocity[1]) + jnp.abs(velocity[2])
                    middles.append(0.25 - 0.5 * size)
                base = lambda m, h, center: cut(gradient[m][h]) + middles[h] * center
                put(rights, stencil(field, s, t, edge, factors, energies, base, coupling), s, t)
        if edge >= 0:
            put_out(s - 1).start()

    each_row(row)
    put_out(CS - 1).start()
    for s in range(CS):
        put_out(s).wait()


def first_body(v, words, owner, right, coupling, fa, fb, fc, fd, out, factor, scaled, ga, gb, gc, gd, placed, rights, span_halo, chord_halo, chord_edge, word_sem, right_sem):
    per_row = owner.shape[1] // CS
    take = lambda s: pltpu.make_async_copy(right.at[:, s], rights.at[:, s], right_sem.at[s])
    landed = lambda s: placed.at[:, pl.ds(pl.multiple_of(s * per_row * 8, 8), per_row * 8)]
    whole = lambda s: pltpu.make_async_copy(landed(s), landed(s), word_sem.at[s])

    def gather(s, carry):
        for j in range(per_row):
            k = s * per_row + j
            pltpu.make_async_copy(
                words.at[owner[0, k]], placed.at[:, pl.ds(pl.multiple_of(k * 8, 8), 8)], word_sem.at[s]
            ).start()
        take(s).start()
        return carry

    lax.fori_loop(0, CS, gather, 0)
    unpack_faces((fa, fb, fc, fd), span_halo, chord_halo)
    clear_padding(chord_edge)
    field = Field(v, span_halo, chord_halo)

    def row(s, edge):
        whole(s).wait()
        take(s).wait()
        for t in range(TILES):
            factors, energies, scales = [], [], []
            for h in range(HALVES):
                pair = [placed[w, pl.ds((s * 8 + t * 2) * 8 + h, 8, stride=2), :] for w in range(2)]
                codes = []
                for word in pair:
                    codes += [(word >> 16).astype(F32), ((word << 16) >> 16).astype(F32)]
                velocity = [codes[a] * (1.0 / VELOCITY_CODE) for a in range(3)]
                size = jnp.abs(velocity[0]) + jnp.abs(velocity[1]) + jnp.abs(velocity[2])
                scale = 1.0 / (1.75 + 0.5 * size)
                half = 0.5 * scale
                pairs = [(half * up, half * low) for up, low in halves_of(velocity, h)]
                energy = (-1.0 / ENERGY_CODE) * codes[3] * half
                factors.append(pairs)
                energies.append(energy)
                scales.append(scale)
                for a in range(3):
                    factor[2 * a, s, rows(t), lanes(h)] = pairs[a][0]
                    factor[2 * a + 1, s, rows(t), lanes(h)] = pairs[a][1]
                factor[6, s, rows(t), lanes(h)] = energy

            def base(m, h, center):
                value = rights[m, s, rows(t), lanes(h)] * scales[h]
                scaled[m, s, rows(t), lanes(h)] = value
                return value

            put(out, stencil(field, s, t, edge, factors, energies, base, coupling), s, t, chord_edge)

    each_row(row)
    pack_faces(out, chord_edge, (ga, gb, gc, gd))


def sweep_row(field, factor, scaled, coupling, out, chord_edge, s, edge):
    for t in range(TILES):
        read = lambda i, h: factor[i, s, rows(t), lanes(h)]
        factors = [[(read(2 * a, h), read(2 * a + 1, h)) for a in range(3)] for h in range(HALVES)]
        energies = [read(6, h) for h in range(HALVES)]
        base = lambda m, h, center: scaled[m, s, rows(t), lanes(h)]
        put(out, stencil(field, s, t, edge, factors, energies, base, coupling), s, t, chord_edge)


def sweep_body(v, factor, scaled, coupling, fa, fb, fc, fd, out, ga, gb, gc, gd, span_halo, chord_halo, chord_edge):
    unpack_faces((fa, fb, fc, fd), span_halo, chord_halo)
    clear_padding(chord_edge)
    field = Field(v, span_halo, chord_halo)
    each_row(lambda s, edge: sweep_row(field, factor, scaled, coupling, out, chord_edge, s, edge))
    pack_faces(out, chord_edge, (ga, gb, gc, gd))


def last_body(v, factor, scaled, coupling, fa, fb, fc, fd, out, cells, span_halo, chord_halo, out_sem):
    unpack_faces((fa, fb, fc, fd), span_halo, chord_halo)
    field = Field(v, span_halo, chord_halo)
    put_out = lambda s: pltpu.make_async_copy(cells.at[:, s], out.at[:, s], out_sem.at[s])

    def row(s, edge):
        sweep_row(field, factor, scaled, coupling, cells, None, s, edge)
        if edge >= 0:
            put_out(s - 1).start()

    each_row(row)
    put_out(CS - 1).start()
    for s in range(CS):
        put_out(s).wait()


BLOCK = (NCONS, CS, CC, CN)
CELLS = (BLOCK, F32)
ROW_SEMS = pltpu.SemaphoreType.DMA((CS,))


def shards(adjoint_next, objective_grad, state_next, checkpoint_pieces, slot_target, piece_owner, coupling):
    outgoing = send_order(checkpoint_pieces, slot_target)
    incoming = lax.all_to_all(outgoing, ("span", "chord"), split_axis=0, concat_axis=0, tiled=True)
    halo = exchange(call(faces_body, FACES, [adjoint_next], scratch=[CHORD_HALO], name="faces", cost=MIB // 2))
    right = call(
        right_body,
        [CELLS],
        [adjoint_next, state_next, objective_grad, coupling, *halo],
        scratch=[
            pltpu.VMEM((NSTATE, CS, CC, CN), BF16),
            pltpu.VMEM(BLOCK, BF16),
            pltpu.VMEM(BLOCK, F32),
            SPAN_HALO,
            CHORD_HALO,
            pltpu.SemaphoreType.DMA((2, CS)),
            ROW_SEMS,
        ],
        smem=(3,),
        hbm=(1, 2),
        hbm_outs=(0,),
        name="right_side",
        cost=9 * MIB,
    )[0]
    adjoint, factor, scaled, *faces = call(
        first_body,
        [CELLS, ((7, CS, CC, CN), F32), CELLS, *FACES],
        [adjoint_next, incoming, piece_owner, right, coupling, *halo],
        scratch=[
            pltpu.VMEM((2, piece_owner.shape[1] * 8, LANES), jnp.int32),
            pltpu.VMEM(BLOCK, F32),
            SPAN_HALO,
            CHORD_HALO,
            CHORD_HALO,
            ROW_SEMS,
            ROW_SEMS,
        ],
        smem=(2, 4),
        hbm=(1, 3),
        name="first_sweep",
        cost=9 * MIB,
    )
    for sweep in range(2, SWEEPS):
        adjoint, *faces = call(
            sweep_body,
            [CELLS, *FACES],
            [adjoint, factor, scaled, coupling, *exchange(faces)],
            scratch=[SPAN_HALO, CHORD_HALO, CHORD_HALO],
            smem=(3,),
            name="sweep",
            cost=9 * MIB,
        )
    return call(
        last_body,
        [CELLS],
        [adjoint, factor, scaled, coupling, *exchange(faces)],
        scratch=[pltpu.VMEM(BLOCK, F32), SPAN_HALO, CHORD_HALO, ROW_SEMS],
        smem=(3,),
        hbm_outs=(0,),
        name="last_sweep",
        cost=9 * MIB,
    )[0]


def solution(mesh):
    placed = (
        P(None, "span", "chord", None),
        P(None, "span", "chord", None),
        P(None, "span", "chord", None),
        P(None, ("span", "chord"), None),
        P(("span", "chord"), None),
        P(("span", "chord"), None),
        P(),
    )
    return jax.shard_map(
        shards,
        mesh=mesh,
        in_specs=placed,
        out_specs=P(None, "span", "chord", None),
        check_vma=False,
    )
```

```python
import jax
import jax.numpy as jnp
from jax import lax
from jax.experimental import pallas as pl
from jax.experimental.pallas import tpu as pltpu
from jax.sharding import PartitionSpec as P

NCONS = 5
NSTATE = 8
CS = 16
CC = 32
CN = 256
SWEEPS = 4
PIECE = 1024
TILES = CC // 8
LANES = 128
HALVES = CN // LANES
VELOCITY_CODE = 4368.0
ENERGY_CODE = 8190.0
ADJOINT_CODE = 5461.0
MIB = 1 << 20
F32 = jnp.float32
BF16 = jnp.bfloat16


def in_space(array, space):
    return pltpu.with_memory_space_constraint(array, space)


def call(body, outs, args, scratch=(), name=None, smem=(), hbm=(), hbm_outs=(), limit=24 * MIB, cost=4 * MIB):
    space = lambda i: pltpu.SMEM if i in smem else pltpu.HBM if i in hbm else pltpu.VMEM
    out_space = lambda i: pltpu.HBM if i in hbm_outs else pltpu.VMEM
    return pl.pallas_call(
        body,
        out_shape=[out_space(i)(shape, dtype) for i, (shape, dtype) in enumerate(outs)],
        in_specs=[pl.BlockSpec(memory_space=space(i)) for i in range(len(args))],
        out_specs=[pl.BlockSpec(memory_space=out_space(i)) for i in range(len(outs))],
        scratch_shapes=list(scratch),
        compiler_params=pltpu.CompilerParams(vmem_limit_bytes=limit),
        cost_estimate=pl.CostEstimate(flops=cost * 8, bytes_accessed=cost, transcendentals=0),
        name=name,
    )(*[a if i in smem else in_space(a, space(i)) for i, a in enumerate(args)])


def lanes(half):
    return pl.ds(half * LANES, LANES)


def rows(tile):
    return pl.ds(tile * 8, 8)


def wide_rows(pair):
    return pl.ds(pair * 16, 16)


def mask_of(dim, value):
    return lax.broadcasted_iota(jnp.int32, (8, LANES), dim) == value


SPAN_FACE = ((NCONS, CC, CN), BF16)
CHORD_FACE = ((CS // 2, 16, CN), BF16)
FACES = [SPAN_FACE, SPAN_FACE, CHORD_FACE, CHORD_FACE]
SPAN_HALO = pltpu.VMEM((2, NCONS, CC, CN), F32)
CHORD_HALO = pltpu.VMEM((2, CS, 8, CN), F32)


def parity(axis):
    return lax.rem(lax.axis_index(axis), 2)


def unpack_faces(faces, span_halo, chord_halo):
    span_a, span_b, chord_a, chord_b = faces
    p = parity("span")
    for face, side in ((span_a, 1 - p), (span_b, p)):
        for m in range(NCONS):
            for pair in range(CC // 16):
                span_halo[side, m, wide_rows(pair), :] = face[m, wide_rows(pair), :].astype(F32)
    p = parity("chord")
    for face, side in ((chord_a, 1 - p), (chord_b, p)):
        for group in range(CS // 2):
            both = face[group].astype(F32)
            chord_halo[side, 2 * group] = both[:8]
            chord_halo[side, 2 * group + 1] = both[8:]


def pack_faces(cells, chord_edge, faces):
    span_a, span_b, chord_a, chord_b = faces
    p = parity("span")
    for face, side in ((span_a, 1 - p), (span_b, p)):
        for m in range(NCONS):
            for pair in range(CC // 16):
                face[m, wide_rows(pair), :] = cells[m, side * (CS - 1), wide_rows(pair), :].astype(BF16)
    p = parity("chord")
    for face, side in ((chord_a, 1 - p), (chord_b, p)):
        for group in range(CS // 2):
            both = [chord_edge[side, 2 * group], chord_edge[side, 2 * group + 1]]
            face[group] = jnp.concatenate(both, axis=0).astype(BF16)


def code_pair(high, low, scale):
    code = lambda x: jnp.round(x * scale).astype(jnp.int32)
    return (code(high) << 16) | (code(low) & 0xFFFF)


def decode_pair(word):
    return (word >> 16).astype(F32), ((word << 16) >> 16).astype(F32)


START_SPAN = ((NCONS, CC // 2, CN), jnp.int32)
START_CHORD = ((CS // 2, 8, CN), jnp.int32)
START_FACES = [START_SPAN, START_SPAN, START_CHORD, START_CHORD]


def pack_start(cells, chord_edge, faces):
    span_a, span_b, chord_a, chord_b = faces
    p = parity("span")
    for face, side in ((span_a, 1 - p), (span_b, p)):
        for m in range(NCONS):
            for pair in range(CC // 16):
                high, low = (cells[m, side * (CS - 1), rows(2 * pair + i), :] for i in range(2))
                face[m, rows(pair), :] = code_pair(high, low, ADJOINT_CODE)
    p = parity("chord")
    for face, side in ((chord_a, 1 - p), (chord_b, p)):
        for group in range(CS // 2):
            face[group] = code_pair(chord_edge[side, 2 * group], chord_edge[side, 2 * group + 1], ADJOINT_CODE)


def unpack_start(faces, span_halo, chord_halo):
    span_a, span_b, chord_a, chord_b = faces
    p = parity("span")
    for face, side in ((span_a, 1 - p), (span_b, p)):
        for m in range(NCONS):
            for pair in range(CC // 16):
                for i, half in enumerate(decode_pair(face[m, rows(pair), :])):
                    span_halo[side, m, rows(2 * pair + i), :] = half * (1.0 / ADJOINT_CODE)
    p = parity("chord")
    for face, side in ((chord_a, 1 - p), (chord_b, p)):
        for group in range(CS // 2):
            for i, half in enumerate(decode_pair(face[group])):
                chord_halo[side, 2 * group + i] = half * (1.0 / ADJOINT_CODE)


def clear_padding(chord_edge):
    for side in range(2):
        for s in range(CS):
            chord_edge[side, s] = jnp.zeros((8, CN), F32)


def faces_body(cells, span_a, span_b, chord_a, chord_b, chord_edge):
    clear_padding(chord_edge)
    for s in range(CS):
        for m in range(NCONS):
            chord_edge[0, s, pl.ds(m, 1), :] = cells[m, s, pl.ds(0, 1), :]
            chord_edge[1, s, pl.ds(m, 1), :] = cells[m, s, pl.ds(CC - 1, 1), :]
    pack_start(cells, chord_edge, (span_a, span_b, chord_a, chord_b))


def exchange(faces):
    def swap(face, axis, start):
        count = lax.axis_size(axis)
        pairs = [(i, i + 1) for i in range(start, count - 1, 2)]
        return lax.ppermute(face, axis, pairs + [(b, a) for a, b in pairs])

    span_a, span_b, chord_a, chord_b = faces
    span_b = swap(span_b, "span", 1)
    span_a = swap(span_a, "span", 0)
    chord_b = swap(chord_b, "chord", 1)
    chord_a = swap(chord_a, "chord", 0)
    return span_a, span_b, chord_a, chord_b


class Field:
    def __init__(self, cells, span_halo=None, chord_halo=None):
        self.cells = cells
        self.span_halo = span_halo
        self.chord_halo = chord_halo

    def center(self, m, s, t, h):
        return self.cells[m, s, rows(t), lanes(h)]

    def span(self, m, s, t, h, step, edge):
        if edge == step and self.span_halo is None:
            return jnp.zeros((8, LANES), F32)
        if edge == step:
            return self.span_halo[1 if step > 0 else 0, m, rows(t), lanes(h)]
        return self.cells[m, s + step, rows(t), lanes(h)]

    def beyond(self, side, m, s, h):
        if self.chord_halo is None:
            return jnp.zeros((8, LANES), F32)
        return jnp.broadcast_to(self.chord_halo[side, s, pl.ds(m, 1), lanes(h)], (8, LANES))

    def chord(self, m, s, t, h, step, center, first, last):
        if step > 0:
            after = self.beyond(1, m, s, h) if t == TILES - 1 else self.center(m, s, t + 1, h)
            return pltpu.roll(jnp.where(first, after, center), 7, 0)
        before = self.beyond(0, m, s, h) if t == 0 else self.center(m, s, t - 1, h)
        return pltpu.roll(jnp.where(last, before, center), 1, 0)


def normal(centers, h, step, lane_first, lane_last):
    if step > 0:
        source = jnp.where(lane_first, centers[h + 1], centers[h]) if h + 1 < HALVES else centers[h]
        return pltpu.roll(source, LANES - 1, 1)
    source = jnp.where(lane_last, centers[h - 1], centers[h]) if h > 0 else centers[h]
    return pltpu.roll(source, 1, 1)


def stencil(field, s, t, edge, factors, energies, bases, coupling):
    row_first, row_last = mask_of(0, 0), mask_of(0, 7)
    lane_first, lane_last = mask_of(1, 0), mask_of(1, LANES - 1)
    centers = [[field.center(m, s, t, h) for h in range(HALVES)] for m in range(NCONS)]
    out = []
    for m in range(NCONS):
        scalars = [coupling[n, m] for n in range(NCONS)]
        pair = []
        for h in range(HALVES):
            (span_up, span_low), (chord_up, chord_low), (normal_up, normal_low) = factors[h]
            mixed = scalars[0] * centers[0][h]
            for n in range(1, NCONS):
                mixed = mixed + scalars[n] * centers[n][h]
            total = bases(m, h, centers[m][h]) + energies[h] * mixed
            total = total + span_up * field.span(m, s, t, h, 1, edge)
            total = total + span_low * field.span(m, s, t, h, -1, edge)
            total = total + chord_up * field.chord(m, s, t, h, 1, centers[m][h], row_first, row_last)
            total = total + chord_low * field.chord(m, s, t, h, -1, centers[m][h], row_first, row_last)
            total = total + normal_up * normal(centers[m], h, 1, lane_first, lane_last)
            total = total + normal_low * normal(centers[m], h, -1, lane_first, lane_last)
            pair.append(total)
        out.append(pair)
    return out


def each_row(row):
    row(0, -1)

    def inner(s, carry):
        row(s, 0)
        return carry

    lax.fori_loop(1, CS - 1, inner, 0)
    row(CS - 1, 1)


def halves_of(velocity, h):
    pairs = []
    for a in range(3):
        up = jnp.maximum(-velocity[a], 0.0) + 0.25
        low = jnp.maximum(velocity[a], 0.0) + 0.25
        if a == 2 and h == HALVES - 1:
            up = jnp.where(mask_of(1, LANES - 1), 0.0, up)
        if a == 2 and h == 0:
            low = jnp.where(mask_of(1, 0), 0.0, low)
        pairs.append((up, low))
    return pairs


def put(out, result, s, t, chord_edge=None):
    for m in range(NCONS):
        for h in range(HALVES):
            tile = result[m][h]
            out[m, s, rows(t), lanes(h)] = tile
            if chord_edge is not None and t == 0:
                chord_edge[0, s, pl.ds(m, 1), lanes(h)] = tile[0:1]
            if chord_edge is not None and t == TILES - 1:
                chord_edge[1, s, pl.ds(m, 1), lanes(h)] = tile[7:8]


SLOTS = 16


def send_body(pieces, target, out, taken, words, ordered, in_sem, out_sem):
    groups = pieces.shape[1] // SLOTS
    take = lambda g: pltpu.make_async_copy(
        pieces.at[:, pl.ds(g * SLOTS, SLOTS)], taken.at[:, pl.ds(g * SLOTS, SLOTS)], in_sem.at[g]
    )
    for g in range(groups):
        take(g).start()

    def group(g, carry):
        take(g).wait()
        for c in range(PIECE // LANES):
            read = lambda f: taken[f, pl.ds(pl.multiple_of(g * SLOTS, SLOTS), SLOTS), lanes(c)].astype(F32)
            ratio = 1.0 / read(0)
            codes = [jnp.round((read(1 + a) * ratio - read(5 + a)) * VELOCITY_CODE).astype(jnp.int32) for a in range(3)]
            codes.append(jnp.round(read(4) * ratio * ENERGY_CODE).astype(jnp.int32))
            for w in range(2):
                word = (codes[2 * w] << 16) | (codes[2 * w + 1] & 0xFFFF)
                for part in range(2):
                    at = pl.multiple_of((g * 2 + part) * 64 + c * 8, 8)
                    words[w, pl.ds(at, 8), :] = word[part * 8 : part * 8 + 8]
        for j in range(SLOTS):
            d = target[0, g * SLOTS + j]
            for w in range(2):
                ordered[d, w] = words[w, pl.ds((g * 2 + j // 8) * 64 + j % 8, 8, stride=8), :]
        return carry

    lax.fori_loop(0, groups, group, 0)
    copy = pltpu.make_async_copy(ordered, out, out_sem)
    copy.start()
    copy.wait()


def send_order(pieces, target):
    count = pieces.shape[1]
    return call(
        send_body,
        [((count, 2, 8, LANES), jnp.int32)],
        [pieces, target],
        scratch=[
            pltpu.VMEM(pieces.shape, BF16),
            pltpu.VMEM((2, count * 8, LANES), jnp.int32),
            pltpu.VMEM((count, 2, 8, LANES), jnp.int32),
            pltpu.SemaphoreType.DMA((count // SLOTS,)),
            pltpu.SemaphoreType.DMA,
        ],
        smem=(1,),
        hbm=(0,),
        hbm_outs=(0,),
        name="send_order",
        cost=3 * MIB,
    )[0]


def right_body(v, state, grad, coupling, out, span_next, chord_next, states, grads, rights, in_sem, out_sem):
    copies = lambda s: (
        pltpu.make_async_copy(state.at[:, s], states.at[:, s], in_sem.at[0, s]),
        pltpu.make_async_copy(grad.at[:, s], grads.at[:, s], in_sem.at[1, s]),
    )
    put_out = lambda s: pltpu.make_async_copy(rights.at[:, s], out.at[:, s], out_sem.at[s])
    for s in range(CS):
        for copy in copies(s):
            copy.start()
    field = Field(v)
    row_first, row_last = mask_of(0, 0), mask_of(0, 7)

    def row(s, edge):
        for copy in copies(s):
            copy.wait()
        for pair in range(TILES // 2):
            wide = lambda ref, f, h: ref[f, s, wide_rows(pair), lanes(h)].astype(F32)
            fields = [[wide(states, f, h) for h in range(HALVES)] for f in range(NSTATE)]
            gradient = [[wide(grads, m, h) for h in range(HALVES)] for m in range(NCONS)]
            for part in range(2):
                t = pair * 2 + part
                cut = lambda x: x[part * 8 : part * 8 + 8]
                factors, energies, middles = [], [], []
                for h in range(HALVES):
                    ratio = 1.0 / cut(fields[0][h])
                    velocity = [cut(fields[1 + a][h]) * ratio - cut(fields[5 + a][h]) for a in range(3)]
                    factors.append([(0.5 * up, 0.5 * low) for up, low in halves_of(velocity, h)])
                    energies.append(-0.5 * (cut(fields[4][h]) * ratio))
                    size = jnp.abs(velocity[0]) + jnp.abs(velocity[1]) + jnp.abs(velocity[2])
                    middles.append(0.25 - 0.5 * size)
                    (span_up, span_low), (chord_up, chord_low), _ = factors[h]
                    if edge == -1:
                        span_next[0, rows(t), lanes(h)] = span_low
                    if edge == 1:
                        span_next[1, rows(t), lanes(h)] = span_up
                    if t == 0:
                        chord_next[0, s, :, lanes(h)] = jnp.where(row_first, chord_low, 0.0)
                    if t == TILES - 1:
                        chord_next[1, s, :, lanes(h)] = jnp.where(row_last, chord_up, 0.0)
                base = lambda m, h, center: cut(gradient[m][h]) + middles[h] * center
                put(rights, stencil(field, s, t, edge, factors, energies, base, coupling), s, t)
        if edge >= 0:
            put_out(s - 1).start()

    each_row(row)
    put_out(CS - 1).start()
    for s in range(CS):
        put_out(s).wait()


def first_body(v, words, owner, right, coupling, span_next, chord_next, fa, fb, fc, fd, out, factor, scaled, ga, gb, gc, gd, placed, rights, span_halo, chord_halo, chord_edge, word_sem, right_sem):
    per_row = owner.shape[1] // CS
    take = lambda s: pltpu.make_async_copy(right.at[:, s], rights.at[:, s], right_sem.at[s])
    landed = lambda s: placed.at[:, pl.ds(pl.multiple_of(s * per_row * 8, 8), per_row * 8)]
    whole = lambda s: pltpu.make_async_copy(landed(s), landed(s), word_sem.at[s])

    def gather(s, carry):
        for j in range(per_row):
            k = s * per_row + j
            pltpu.make_async_copy(
                words.at[owner[0, k]], placed.at[:, pl.ds(pl.multiple_of(k * 8, 8), 8)], word_sem.at[s]
            ).start()
        take(s).start()
        return carry

    lax.fori_loop(0, CS, gather, 0)
    unpack_start((fa, fb, fc, fd), span_halo, chord_halo)
    clear_padding(chord_edge)
    field = Field(v, span_halo, chord_halo)

    def row(s, edge):
        whole(s).wait()
        take(s).wait()
        for t in range(TILES):
            factors, energies, scales = [], [], []
            for h in range(HALVES):
                pair = [placed[w, pl.ds((s * 8 + t * 2) * 8 + h, 8, stride=2), :] for w in range(2)]
                codes = [*decode_pair(pair[0]), *decode_pair(pair[1])]
                velocity = [codes[a] * (1.0 / VELOCITY_CODE) for a in range(3)]
                size = jnp.abs(velocity[0]) + jnp.abs(velocity[1]) + jnp.abs(velocity[2])
                scale = 1.0 / (1.75 + 0.5 * size)
                half = 0.5 * scale
                pairs = [(half * up, half * low) for up, low in halves_of(velocity, h)]
                energy = (-1.0 / ENERGY_CODE) * codes[3] * half
                factors.append(pairs)
                energies.append(energy)
                scales.append(scale)
                for a in range(3):
                    factor[2 * a, s, rows(t), lanes(h)] = pairs[a][0]
                    factor[2 * a + 1, s, rows(t), lanes(h)] = pairs[a][1]
                factor[6, s, rows(t), lanes(h)] = energy

            def base(m, h, center):
                value = rights[m, s, rows(t), lanes(h)]
                if edge != 0:
                    side = 0 if edge == -1 else 1
                    value = value + span_next[side, rows(t), lanes(h)] * span_halo[side, m, rows(t), lanes(h)]
                if t == 0:
                    value = value + chord_next[0, s, :, lanes(h)] * field.beyond(0, m, s, h)
                if t == TILES - 1:
                    value = value + chord_next[1, s, :, lanes(h)] * field.beyond(1, m, s, h)
                value = value * scales[h]
                scaled[m, s, rows(t), lanes(h)] = value
                return value

            put(out, stencil(field, s, t, edge, factors, energies, base, coupling), s, t, chord_edge)

    each_row(row)
    pack_faces(out, chord_edge, (ga, gb, gc, gd))


def sweep_row(field, factor, scaled, coupling, out, chord_edge, s, edge):
    for t in range(TILES):
        read = lambda i, h: factor[i, s, rows(t), lanes(h)]
        factors = [[(read(2 * a, h), read(2 * a + 1, h)) for a in range(3)] for h in range(HALVES)]
        energies = [read(6, h) for h in range(HALVES)]
        base = lambda m, h, center: scaled[m, s, rows(t), lanes(h)]
        put(out, stencil(field, s, t, edge, factors, energies, base, coupling), s, t, chord_edge)


def sweep_body(v, factor, scaled, coupling, fa, fb, fc, fd, out, ga, gb, gc, gd, span_halo, chord_halo, chord_edge):
    unpack_faces((fa, fb, fc, fd), span_halo, chord_halo)
    clear_padding(chord_edge)
    field = Field(v, span_halo, chord_halo)
    each_row(lambda s, edge: sweep_row(field, factor, scaled, coupling, out, chord_edge, s, edge))
    pack_faces(out, chord_edge, (ga, gb, gc, gd))


def last_body(v, factor, scaled, coupling, fa, fb, fc, fd, out, cells, span_halo, chord_halo, out_sem):
    unpack_faces((fa, fb, fc, fd), span_halo, chord_halo)
    field = Field(v, span_halo, chord_halo)
    put_out = lambda s: pltpu.make_async_copy(cells.at[:, s], out.at[:, s], out_sem.at[s])

    def row(s, edge):
        sweep_row(field, factor, scaled, coupling, cells, None, s, edge)
        if edge >= 0:
            put_out(s - 1).start()

    each_row(row)
    put_out(CS - 1).start()
    for s in range(CS):
        put_out(s).wait()


BLOCK = (NCONS, CS, CC, CN)
CELLS = (BLOCK, F32)
ROW_SEMS = pltpu.SemaphoreType.DMA((CS,))


def shards(adjoint_next, objective_grad, state_next, checkpoint_pieces, slot_target, piece_owner, coupling):
    outgoing = send_order(checkpoint_pieces, slot_target)
    incoming = lax.all_to_all(outgoing, ("span", "chord"), split_axis=0, concat_axis=0, tiled=True)
    halo = exchange(call(faces_body, START_FACES, [adjoint_next], scratch=[CHORD_HALO], name="faces", cost=MIB // 2))
    right, span_next, chord_next = call(
        right_body,
        [CELLS, ((2, CC, CN), F32), ((2, CS, 8, CN), F32)],
        [adjoint_next, state_next, objective_grad, coupling],
        scratch=[
            pltpu.VMEM((NSTATE, CS, CC, CN), BF16),
            pltpu.VMEM(BLOCK, BF16),
            pltpu.VMEM(BLOCK, F32),
            pltpu.SemaphoreType.DMA((2, CS)),
            ROW_SEMS,
        ],
        smem=(3,),
        hbm=(1, 2),
        hbm_outs=(0,),
        name="right_side",
        cost=9 * MIB,
    )
    adjoint, factor, scaled, *faces = call(
        first_body,
        [CELLS, ((7, CS, CC, CN), F32), CELLS, *FACES],
        [adjoint_next, incoming, piece_owner, right, coupling, span_next, chord_next, *halo],
        scratch=[
            pltpu.VMEM((2, piece_owner.shape[1] * 8, LANES), jnp.int32),
            pltpu.VMEM(BLOCK, F32),
            SPAN_HALO,
            CHORD_HALO,
            CHORD_HALO,
            ROW_SEMS,
            ROW_SEMS,
        ],
        smem=(2, 4),
        hbm=(1, 3),
        name="first_sweep",
        cost=9 * MIB,
    )
    for sweep in range(2, SWEEPS):
        adjoint, *faces = call(
            sweep_body,
            [CELLS, *FACES],
            [adjoint, factor, scaled, coupling, *exchange(faces)],
            scratch=[SPAN_HALO, CHORD_HALO, CHORD_HALO],
            smem=(3,),
            name="sweep",
            cost=9 * MIB,
        )
    return call(
        last_body,
        [CELLS],
        [adjoint, factor, scaled, coupling, *exchange(faces)],
        scratch=[pltpu.VMEM(BLOCK, F32), SPAN_HALO, CHORD_HALO, ROW_SEMS],
        smem=(3,),
        hbm_outs=(0,),
        name="last_sweep",
        cost=9 * MIB,
    )[0]


def solution(mesh):
    placed = (
        P(None, "span", "chord", None),
        P(None, "span", "chord", None),
        P(None, "span", "chord", None),
        P(None, ("span", "chord"), None),
        P(("span", "chord"), None),
        P(("span", "chord"), None),
        P(),
    )
    return jax.shard_map(
        shards,
        mesh=mesh,
        in_specs=placed,
        out_specs=P(None, "span", "chord", None),
        check_vma=False,
    )
```

```python
import jax
import jax.numpy as jnp
from jax import lax
from jax.experimental import pallas as pl
from jax.experimental.pallas import tpu as pltpu
from jax.sharding import PartitionSpec as P

NCONS = 5
NSTATE = 8
CS = 16
CC = 32
CN = 256
SWEEPS = 4
PIECE = 1024
TILES = CC // 8
LANES = 128
HALVES = CN // LANES
VELOCITY_CODE = 4368.0
ENERGY_CODE = 8190.0
ADJOINT_CODE = 5461.0
MIB = 1 << 20
F32 = jnp.float32
BF16 = jnp.bfloat16


def in_space(array, space):
    return pltpu.with_memory_space_constraint(array, space)


def call(body, outs, args, scratch=(), smem=(), hbm=(), hbm_outs=(), aliases=None, limit=24 * MIB, cost=4 * MIB):
    space = lambda i: pltpu.SMEM if i in smem else pltpu.HBM if i in hbm else pltpu.VMEM
    out_space = lambda i: pltpu.HBM if i in hbm_outs else pltpu.VMEM
    return pl.pallas_call(
        body,
        out_shape=[out_space(i)(shape, dtype) for i, (shape, dtype) in enumerate(outs)],
        in_specs=[pl.BlockSpec(memory_space=space(i)) for i in range(len(args))],
        out_specs=[pl.BlockSpec(memory_space=out_space(i)) for i in range(len(outs))],
        scratch_shapes=list(scratch),
        input_output_aliases=aliases or {},
        compiler_params=pltpu.CompilerParams(vmem_limit_bytes=limit),
        cost_estimate=pl.CostEstimate(flops=cost * 8, bytes_accessed=cost, transcendentals=0),
    )(*[a if i in smem else in_space(a, space(i)) for i, a in enumerate(args)])


def lanes(half):
    return pl.ds(half * LANES, LANES)


def rows(tile):
    return pl.ds(tile * 8, 8)


def wide_rows(pair):
    return pl.ds(pair * 16, 16)


def mask_of(dim, value):
    return lax.broadcasted_iota(jnp.int32, (8, LANES), dim) == value


SPAN_FACE = ((NCONS, CC, CN), BF16)
CHORD_FACE = ((CS // 2, 16, CN), BF16)
FACES = [CHORD_FACE, CHORD_FACE, SPAN_FACE, SPAN_FACE]
SPAN_HALO = pltpu.VMEM((2, NCONS, CC, CN), F32)
CHORD_HALO = pltpu.VMEM((2, CS, 8, CN), F32)


def parity(axis):
    return lax.rem(lax.axis_index(axis), 2)


def unpack_span(faces, span_halo):
    p = parity("span")
    for face, side in zip(faces, (1 - p, p)):
        for m in range(NCONS):
            for pair in range(CC // 16):
                span_halo[side, m, wide_rows(pair), :] = face[m, wide_rows(pair), :].astype(F32)


def unpack_chord(faces, chord_halo, groups=range(CS // 2)):
    p = parity("chord")
    for face, side in zip(faces, (1 - p, p)):
        for group in groups:
            both = face[group].astype(F32)
            chord_halo[side, 2 * group] = both[:8]
            chord_halo[side, 2 * group + 1] = both[8:]


def pack_faces(cells, chord_edge, faces):
    chord_b, chord_a, span_b, span_a = faces
    p = parity("span")
    for face, side in ((span_a, 1 - p), (span_b, p)):
        for m in range(NCONS):
            for pair in range(CC // 16):
                face[m, wide_rows(pair), :] = cells[m, side * (CS - 1), wide_rows(pair), :].astype(BF16)
    p = parity("chord")
    for face, side in ((chord_a, 1 - p), (chord_b, p)):
        for group in range(CS // 2):
            both = [chord_edge[side, 2 * group], chord_edge[side, 2 * group + 1]]
            face[group] = jnp.concatenate(both, axis=0).astype(BF16)


def code_pair(high, low, scale):
    code = lambda x: jnp.round(x * scale).astype(jnp.int32)
    return (code(high) << 16) | (code(low) & 0xFFFF)


def decode_pair(word):
    return (word >> 16).astype(F32), ((word << 16) >> 16).astype(F32)


START_SPAN = ((NCONS, CC // 2, CN), jnp.int32)
START_CHORD = ((CS // 2, 8, CN), jnp.int32)
START_FACES = [START_CHORD, START_CHORD, START_SPAN, START_SPAN]


def pack_start(cells, chord_edge, faces):
    chord_b, chord_a, span_b, span_a = faces
    p = parity("span")
    for face, side in ((span_a, 1 - p), (span_b, p)):
        for m in range(NCONS):
            for pair in range(CC // 16):
                high, low = (cells[m, side * (CS - 1), rows(2 * pair + i), :] for i in range(2))
                face[m, rows(pair), :] = code_pair(high, low, ADJOINT_CODE)
    p = parity("chord")
    for face, side in ((chord_a, 1 - p), (chord_b, p)):
        for group in range(CS // 2):
            face[group] = code_pair(chord_edge[side, 2 * group], chord_edge[side, 2 * group + 1], ADJOINT_CODE)


def unpack_start(faces, span_halo, chord_halo):
    chord_b, chord_a, span_b, span_a = faces
    p = parity("span")
    for face, side in ((span_a, 1 - p), (span_b, p)):
        for m in range(NCONS):
            for pair in range(CC // 16):
                for i, half in enumerate(decode_pair(face[m, rows(pair), :])):
                    span_halo[side, m, rows(2 * pair + i), :] = half * (1.0 / ADJOINT_CODE)
    p = parity("chord")
    for face, side in ((chord_a, 1 - p), (chord_b, p)):
        for group in range(CS // 2):
            for i, half in enumerate(decode_pair(face[group])):
                chord_halo[side, 2 * group + i] = half * (1.0 / ADJOINT_CODE)


def clear_padding(chord_edge):
    for side in range(2):
        for s in range(CS):
            chord_edge[side, s] = jnp.zeros((8, CN), F32)


def faces_body(cells, chord_b, chord_a, span_b, span_a, chord_edge):
    clear_padding(chord_edge)
    for s in range(CS):
        for m in range(NCONS):
            chord_edge[0, s, pl.ds(m, 1), :] = cells[m, s, pl.ds(0, 1), :]
            chord_edge[1, s, pl.ds(m, 1), :] = cells[m, s, pl.ds(CC - 1, 1), :]
    pack_start(cells, chord_edge, (chord_b, chord_a, span_b, span_a))


def exchange(faces):
    def swap(face, axis, start):
        count = lax.axis_size(axis)
        pairs = [(i, i + 1) for i in range(start, count - 1, 2)]
        return lax.ppermute(face, axis, pairs + [(b, a) for a, b in pairs])

    chord_b, chord_a, span_b, span_a = faces
    return swap(chord_b, "chord", 1), swap(chord_a, "chord", 0), swap(span_b, "span", 1), swap(span_a, "span", 0)


class Field:
    def __init__(self, cells, span_halo=None, chord_halo=None):
        self.cells = cells
        self.span_halo = span_halo
        self.chord_halo = chord_halo

    def center(self, m, s, t, h):
        return self.cells[m, s, rows(t), lanes(h)]

    def span(self, m, s, t, h, step, edge):
        if edge == step and self.span_halo is None:
            return jnp.zeros((8, LANES), F32)
        if edge == step:
            return self.span_halo[1 if step > 0 else 0, m, rows(t), lanes(h)]
        return self.cells[m, s + step, rows(t), lanes(h)]

    def beyond(self, side, m, s, h):
        if self.chord_halo is None:
            return jnp.zeros((8, LANES), F32)
        return jnp.broadcast_to(self.chord_halo[side, s, pl.ds(m, 1), lanes(h)], (8, LANES))

    def chord(self, m, s, t, h, step, center, first, last):
        if step > 0:
            after = self.beyond(1, m, s, h) if t == TILES - 1 else self.center(m, s, t + 1, h)
            return pltpu.roll(jnp.where(first, after, center), 7, 0)
        before = self.beyond(0, m, s, h) if t == 0 else self.center(m, s, t - 1, h)
        return pltpu.roll(jnp.where(last, before, center), 1, 0)


def normal(centers, h, step, lane_first, lane_last):
    if step > 0:
        source = jnp.where(lane_first, centers[h + 1], centers[h]) if h + 1 < HALVES else centers[h]
        return pltpu.roll(source, LANES - 1, 1)
    source = jnp.where(lane_last, centers[h - 1], centers[h]) if h > 0 else centers[h]
    return pltpu.roll(source, 1, 1)


def stencil(field, s, t, edge, factors, energies, bases, coupling):
    row_first, row_last = mask_of(0, 0), mask_of(0, 7)
    lane_first, lane_last = mask_of(1, 0), mask_of(1, LANES - 1)
    centers = [[field.center(m, s, t, h) for h in range(HALVES)] for m in range(NCONS)]
    out = []
    for m in range(NCONS):
        scalars = [coupling[n, m] for n in range(NCONS)]
        pair = []
        for h in range(HALVES):
            (span_up, span_low), (chord_up, chord_low), (normal_up, normal_low) = factors[h]
            mixed = scalars[0] * centers[0][h]
            for n in range(1, NCONS):
                mixed = mixed + scalars[n] * centers[n][h]
            total = bases(m, h, centers[m][h]) + energies[h] * mixed
            total = total + span_up * field.span(m, s, t, h, 1, edge)
            total = total + span_low * field.span(m, s, t, h, -1, edge)
            total = total + chord_up * field.chord(m, s, t, h, 1, centers[m][h], row_first, row_last)
            total = total + chord_low * field.chord(m, s, t, h, -1, centers[m][h], row_first, row_last)
            total = total + normal_up * normal(centers[m], h, 1, lane_first, lane_last)
            total = total + normal_low * normal(centers[m], h, -1, lane_first, lane_last)
            pair.append(total)
        out.append(pair)
    return out


def inner_rows(row):
    def inner(s, carry):
        row(s, 0)
        return carry

    lax.fori_loop(1, CS - 1, inner, 0)


def each_row(row):
    row(0, -1)
    inner_rows(row)
    row(CS - 1, 1)


def halves_of(velocity, h):
    pairs = []
    for a in range(3):
        up = jnp.maximum(-velocity[a], 0.0) + 0.25
        low = jnp.maximum(velocity[a], 0.0) + 0.25
        if a == 2 and h == HALVES - 1:
            up = jnp.where(mask_of(1, LANES - 1), 0.0, up)
        if a == 2 and h == 0:
            low = jnp.where(mask_of(1, 0), 0.0, low)
        pairs.append((up, low))
    return pairs


def put(out, result, s, t, chord_edge=None):
    for m in range(NCONS):
        for h in range(HALVES):
            tile = result[m][h]
            out[m, s, rows(t), lanes(h)] = tile
            if chord_edge is not None and t == 0:
                chord_edge[0, s, pl.ds(m, 1), lanes(h)] = tile[0:1]
            if chord_edge is not None and t == TILES - 1:
                chord_edge[1, s, pl.ds(m, 1), lanes(h)] = tile[7:8]


SLOTS = 16


def send_body(pieces, target, out, taken, words, ordered, in_sem, out_sem):
    groups = pieces.shape[1] // SLOTS
    take = lambda g: pltpu.make_async_copy(
        pieces.at[:, pl.ds(g * SLOTS, SLOTS)], taken.at[:, pl.ds(g * SLOTS, SLOTS)], in_sem.at[g]
    )
    for g in range(groups):
        take(g).start()

    def group(g, carry):
        take(g).wait()
        for c in range(PIECE // LANES):
            read = lambda f: taken[f, pl.ds(pl.multiple_of(g * SLOTS, SLOTS), SLOTS), lanes(c)].astype(F32)
            ratio = 1.0 / read(0)
            codes = [jnp.round((read(1 + a) * ratio - read(5 + a)) * VELOCITY_CODE).astype(jnp.int32) for a in range(3)]
            codes.append(jnp.round(read(4) * ratio * ENERGY_CODE).astype(jnp.int32))
            for w in range(2):
                word = (codes[2 * w] << 16) | (codes[2 * w + 1] & 0xFFFF)
                for part in range(2):
                    at = pl.multiple_of((g * 2 + part) * 64 + c * 8, 8)
                    words[w, pl.ds(at, 8), :] = word[part * 8 : part * 8 + 8]
        for j in range(SLOTS):
            d = target[0, g * SLOTS + j]
            for w in range(2):
                ordered[d, w] = words[w, pl.ds((g * 2 + j // 8) * 64 + j % 8, 8, stride=8), :]
        return carry

    lax.fori_loop(0, groups, group, 0)
    copy = pltpu.make_async_copy(ordered, out, out_sem)
    copy.start()
    copy.wait()


def send_order(pieces, target):
    count = pieces.shape[1]
    return call(
        send_body,
        [((count, 2, 8, LANES), jnp.int32)],
        [pieces, target],
        scratch=[
            pltpu.VMEM(pieces.shape, BF16),
            pltpu.VMEM((2, count * 8, LANES), jnp.int32),
            pltpu.VMEM((count, 2, 8, LANES), jnp.int32),
            pltpu.SemaphoreType.DMA((count // SLOTS,)),
            pltpu.SemaphoreType.DMA,
        ],
        smem=(1,),
        hbm=(0,),
        hbm_outs=(0,),
        cost=3 * MIB,
    )[0]


def right_body(v, state, grad, coupling, out, span_next, chord_next, states, grads, rights, in_sem, out_sem):
    copies = lambda s: (
        pltpu.make_async_copy(state.at[:, s], states.at[:, s], in_sem.at[0, s]),
        pltpu.make_async_copy(grad.at[:, s], grads.at[:, s], in_sem.at[1, s]),
    )
    put_out = lambda s: pltpu.make_async_copy(rights.at[:, s], out.at[:, s], out_sem.at[s])
    for s in range(CS):
        for copy in copies(s):
            copy.start()
    field = Field(v)
    row_first, row_last = mask_of(0, 0), mask_of(0, 7)

    def row(s, edge):
        for copy in copies(s):
            copy.wait()
        for pair in range(TILES // 2):
            wide = lambda ref, f, h: ref[f, s, wide_rows(pair), lanes(h)].astype(F32)
            fields = [[wide(states, f, h) for h in range(HALVES)] for f in range(NSTATE)]
            gradient = [[wide(grads, m, h) for h in range(HALVES)] for m in range(NCONS)]
            for part in range(2):
                t = pair * 2 + part
                cut = lambda x: x[part * 8 : part * 8 + 8]
                factors, energies, middles = [], [], []
                for h in range(HALVES):
                    ratio = 1.0 / cut(fields[0][h])
                    velocity = [cut(fields[1 + a][h]) * ratio - cut(fields[5 + a][h]) for a in range(3)]
                    factors.append([(0.5 * up, 0.5 * low) for up, low in halves_of(velocity, h)])
                    energies.append(-0.5 * (cut(fields[4][h]) * ratio))
                    size = jnp.abs(velocity[0]) + jnp.abs(velocity[1]) + jnp.abs(velocity[2])
                    middles.append(0.25 - 0.5 * size)
                    (span_up, span_low), (chord_up, chord_low), _ = factors[h]
                    if edge == -1:
                        span_next[0, rows(t), lanes(h)] = span_low
                    if edge == 1:
                        span_next[1, rows(t), lanes(h)] = span_up
                    if t == 0:
                        chord_next[0, s, :, lanes(h)] = jnp.where(row_first, chord_low, 0.0)
                    if t == TILES - 1:
                        chord_next[1, s, :, lanes(h)] = jnp.where(row_last, chord_up, 0.0)
                base = lambda m, h, center: cut(gradient[m][h]) + middles[h] * center
                put(rights, stencil(field, s, t, edge, factors, energies, base, coupling), s, t)
        if edge >= 0:
            put_out(s - 1).start()

    each_row(row)
    put_out(CS - 1).start()
    for s in range(CS):
        put_out(s).wait()


def first_body(v, words, owner, right, coupling, span_next, chord_next, fa, fb, fc, fd, out, factor, scaled, ga, gb, gc, gd, placed, rights, span_halo, chord_halo, chord_edge, word_sem, right_sem):
    per_row = owner.shape[1] // CS
    take = lambda s: pltpu.make_async_copy(right.at[:, s], rights.at[:, s], right_sem.at[s])
    landed = lambda s: placed.at[:, pl.ds(pl.multiple_of(s * per_row * 8, 8), per_row * 8)]
    whole = lambda s: pltpu.make_async_copy(landed(s), landed(s), word_sem.at[s])

    def gather(s, carry):
        for j in range(per_row):
            k = s * per_row + j
            pltpu.make_async_copy(
                words.at[owner[0, k]], placed.at[:, pl.ds(pl.multiple_of(k * 8, 8), 8)], word_sem.at[s]
            ).start()
        take(s).start()
        return carry

    lax.fori_loop(0, CS, gather, 0)
    unpack_start((fa, fb, fc, fd), span_halo, chord_halo)
    clear_padding(chord_edge)
    field = Field(v, span_halo, chord_halo)

    def row(s, edge):
        whole(s).wait()
        take(s).wait()
        for t in range(TILES):
            factors, energies, scales = [], [], []
            for h in range(HALVES):
                pair = [placed[w, pl.ds((s * 8 + t * 2) * 8 + h, 8, stride=2), :] for w in range(2)]
                codes = [*decode_pair(pair[0]), *decode_pair(pair[1])]
                velocity = [codes[a] * (1.0 / VELOCITY_CODE) for a in range(3)]
                size = jnp.abs(velocity[0]) + jnp.abs(velocity[1]) + jnp.abs(velocity[2])
                scale = 1.0 / (1.75 + 0.5 * size)
                half = 0.5 * scale
                pairs = [(half * up, half * low) for up, low in halves_of(velocity, h)]
                energy = (-1.0 / ENERGY_CODE) * codes[3] * half
                factors.append(pairs)
                energies.append(energy)
                scales.append(scale)
                for a in range(3):
                    factor[2 * a, s, rows(t), lanes(h)] = pairs[a][0]
                    factor[2 * a + 1, s, rows(t), lanes(h)] = pairs[a][1]
                factor[6, s, rows(t), lanes(h)] = energy

            def base(m, h, center):
                value = rights[m, s, rows(t), lanes(h)]
                if edge != 0:
                    side = 0 if edge == -1 else 1
                    value = value + span_next[side, rows(t), lanes(h)] * span_halo[side, m, rows(t), lanes(h)]
                if t == 0:
                    value = value + chord_next[0, s, :, lanes(h)] * field.beyond(0, m, s, h)
                if t == TILES - 1:
                    value = value + chord_next[1, s, :, lanes(h)] * field.beyond(1, m, s, h)
                value = value * scales[h]
                scaled[m, s, rows(t), lanes(h)] = value
                return value

            put(out, stencil(field, s, t, edge, factors, energies, base, coupling), s, t, chord_edge)

    each_row(row)
    pack_faces(out, chord_edge, (ga, gb, gc, gd))


def sweep_row(field, factor, scaled, coupling, out, chord_edge, s, edge):
    for t in range(TILES):
        read = lambda i, h: factor[i, s, rows(t), lanes(h)]
        factors = [[(read(2 * a, h), read(2 * a + 1, h)) for a in range(3)] for h in range(HALVES)]
        energies = [read(6, h) for h in range(HALVES)]
        base = lambda m, h, center: scaled[m, s, rows(t), lanes(h)]
        put(out, stencil(field, s, t, edge, factors, energies, base, coupling), s, t, chord_edge)


def inner_body(v, factor, scaled, coupling, fc, fd, out, chord_edge, chord_halo):
    unpack_chord((fc, fd), chord_halo)
    clear_padding(chord_edge)
    field = Field(v, None, chord_halo)
    inner_rows(lambda s, edge: sweep_row(field, factor, scaled, coupling, out, chord_edge, s, edge))


def ends_body(v, factor, scaled, coupling, fc, fd, fa, fb, before, before_edge, out, chord_edge, ga, gb, gc, gd, span_halo, chord_halo):
    unpack_chord((fc, fd), chord_halo, (0, CS // 2 - 1))
    unpack_span((fa, fb), span_halo)
    field = Field(v, span_halo, chord_halo)
    for s, edge in ((0, -1), (CS - 1, 1)):
        sweep_row(field, factor, scaled, coupling, out, chord_edge, s, edge)
    pack_faces(out, chord_edge, (ga, gb, gc, gd))


def last_inner_body(v, factor, scaled, coupling, fc, fd, out, cells, chord_halo, out_sem):
    unpack_chord((fc, fd), chord_halo)
    field = Field(v, None, chord_halo)
    put_out = lambda s: pltpu.make_async_copy(cells.at[:, s], out.at[:, s], out_sem.at[s])

    def row(s, edge):
        sweep_row(field, factor, scaled, coupling, cells, None, s, edge)
        put_out(s).start()

    inner_rows(row)
    for s in range(1, CS - 1):
        put_out(s).wait()


def last_ends_body(v, factor, scaled, coupling, fc, fd, fa, fb, before, out, cells, span_halo, chord_halo, out_sem):
    unpack_chord((fc, fd), chord_halo, (0, CS // 2 - 1))
    unpack_span((fa, fb), span_halo)
    field = Field(v, span_halo, chord_halo)
    put_out = lambda s: pltpu.make_async_copy(cells.at[:, s], out.at[:, s], out_sem.at[s])
    for s, edge in ((0, -1), (CS - 1, 1)):
        sweep_row(field, factor, scaled, coupling, cells, None, s, edge)
        put_out(s).start()
    for s in (0, CS - 1):
        put_out(s).wait()


BLOCK = (NCONS, CS, CC, CN)
CELLS = (BLOCK, F32)
EDGES = ((2, CS, 8, CN), F32)
ROW_SEMS = pltpu.SemaphoreType.DMA((CS,))


def shards(adjoint_next, objective_grad, state_next, checkpoint_pieces, slot_target, piece_owner, coupling):
    outgoing = send_order(checkpoint_pieces, slot_target)
    incoming = lax.all_to_all(outgoing, ("span", "chord"), split_axis=0, concat_axis=0, tiled=True)
    halo = exchange(call(faces_body, START_FACES, [adjoint_next], scratch=[CHORD_HALO], cost=MIB // 2))
    right, span_next, chord_next = call(
        right_body,
        [CELLS, ((2, CC, CN), F32), ((2, CS, 8, CN), F32)],
        [adjoint_next, state_next, objective_grad, coupling],
        scratch=[
            pltpu.VMEM((NSTATE, CS, CC, CN), BF16),
            pltpu.VMEM(BLOCK, BF16),
            pltpu.VMEM(BLOCK, F32),
            pltpu.SemaphoreType.DMA((2, CS)),
            ROW_SEMS,
        ],
        smem=(3,),
        hbm=(1, 2),
        hbm_outs=(0,),
        cost=9 * MIB,
    )
    adjoint, factor, scaled, *faces = call(
        first_body,
        [CELLS, ((7, CS, CC, CN), F32), CELLS, *FACES],
        [adjoint_next, incoming, piece_owner, right, coupling, span_next, chord_next, *halo],
        scratch=[
            pltpu.VMEM((2, piece_owner.shape[1] * 8, LANES), jnp.int32),
            pltpu.VMEM(BLOCK, F32),
            SPAN_HALO,
            CHORD_HALO,
            CHORD_HALO,
            ROW_SEMS,
            ROW_SEMS,
        ],
        smem=(2, 4),
        hbm=(1, 3),
        cost=9 * MIB,
    )
    for sweep in range(2, SWEEPS + 1):
        last = sweep == SWEEPS
        chord_b, chord_a, span_b, span_a = exchange(faces)
        known = [adjoint, factor, scaled, coupling, chord_a, chord_b]
        if last:
            inner = call(
                last_inner_body,
                [CELLS],
                known,
                scratch=[pltpu.VMEM(BLOCK, F32), CHORD_HALO, ROW_SEMS],
                smem=(3,),
                hbm_outs=(0,),
                cost=8 * MIB,
            )
            return call(
                last_ends_body,
                [CELLS],
                [*known, span_a, span_b, *inner],
                scratch=[pltpu.VMEM(BLOCK, F32), SPAN_HALO, CHORD_HALO, ROW_SEMS],
                smem=(3,),
                hbm=(8,),
                hbm_outs=(0,),
                aliases={8: 0},
                cost=MIB,
            )[0]
        inner = call(inner_body, [CELLS, EDGES], known, scratch=[CHORD_HALO], smem=(3,), cost=8 * MIB)
        adjoint, _, *faces = call(
            ends_body,
            [CELLS, EDGES, *FACES],
            [*known, span_a, span_b, *inner],
            scratch=[SPAN_HALO, CHORD_HALO],
            smem=(3,),
            aliases={8: 0, 9: 1},
            cost=MIB,
        )


def solution(mesh):
    placed = (
        P(None, "span", "chord", None),
        P(None, "span", "chord", None),
        P(None, "span", "chord", None),
        P(None, ("span", "chord"), None),
        P(("span", "chord"), None),
        P(("span", "chord"), None),
        P(),
    )
    return jax.shard_map(
        shards,
        mesh=mesh,
        in_specs=placed,
        out_specs=P(None, "span", "chord", None),
        check_vma=False,
    )
```

```python
import jax
import jax.numpy as jnp
from jax import lax
from jax.experimental import pallas as pl
from jax.experimental.pallas import tpu as pltpu
from jax.sharding import PartitionSpec as P

NCONS = 5
NSTATE = 8
CS = 16
CC = 32
CN = 256
SWEEPS = 4
PIECE = 1024
TILES = CC // 8
LANES = 128
HALVES = CN // LANES
VELOCITY_CODE = 4368.0
ENERGY_CODE = 8190.0
ADJOINT_CODE = 5461.0
MIB = 1 << 20
F32 = jnp.float32
BF16 = jnp.bfloat16


def in_space(array, space):
    return pltpu.with_memory_space_constraint(array, space)


def call(body, outs, args, scratch=(), smem=(), hbm=(), hbm_outs=(), aliases=None, limit=24 * MIB, cost=4 * MIB):
    space = lambda i: pltpu.SMEM if i in smem else pltpu.HBM if i in hbm else pltpu.VMEM
    out_space = lambda i: pltpu.HBM if i in hbm_outs else pltpu.VMEM
    return pl.pallas_call(
        body,
        out_shape=[out_space(i)(shape, dtype) for i, (shape, dtype) in enumerate(outs)],
        in_specs=[pl.BlockSpec(memory_space=space(i)) for i in range(len(args))],
        out_specs=[pl.BlockSpec(memory_space=out_space(i)) for i in range(len(outs))],
        scratch_shapes=list(scratch),
        input_output_aliases=aliases or {},
        compiler_params=pltpu.CompilerParams(vmem_limit_bytes=limit),
        cost_estimate=pl.CostEstimate(flops=cost * 8, bytes_accessed=cost, transcendentals=0),
    )(*[a if i in smem else in_space(a, space(i)) for i, a in enumerate(args)])


def lanes(half):
    return pl.ds(half * LANES, LANES)


def rows(tile):
    return pl.ds(tile * 8, 8)


def wide_rows(pair):
    return pl.ds(pair * 16, 16)


def mask_of(dim, value):
    return lax.broadcasted_iota(jnp.int32, (8, LANES), dim) == value


HOME = 8
FIELD = ((NCONS, CS, HALVES, CC + 2 * HOME, LANES), F32)
FIELD_SCRATCH = pltpu.VMEM(*FIELD)


def chord_rows(t, step=0):
    return pl.ds(HOME + t * 8 + step, 8)


BEYOND = (HOME - 1, HOME + CC)


SPAN_FACE = ((NCONS, CC, CN), BF16)
CHORD_FACE = ((CS // 2, 16, CN), BF16)
FACES = [CHORD_FACE, CHORD_FACE, SPAN_FACE, SPAN_FACE]
SPAN_HALO = pltpu.VMEM((2, NCONS, CC, CN), F32)
EDGES = ((2, CS, 8, CN), F32)
CHORD_HALO = pltpu.VMEM(*EDGES)


def parity(axis):
    return lax.rem(lax.axis_index(axis), 2)


def unpack_span(faces, span_halo):
    p = parity("span")
    for face, side in zip(faces, (1 - p, p)):
        for m in range(NCONS):
            for pair in range(CC // 16):
                span_halo[side, m, wide_rows(pair), :] = face[m, wide_rows(pair), :].astype(F32)


def pack_span(field, faces):
    p = parity("span")
    for face, side in zip(faces, (1 - p, p)):
        for m in range(NCONS):
            for pair in range(CC // 16):
                for h in range(HALVES):
                    cells = field[m, side * (CS - 1), h, pl.ds(HOME + pair * 16, 16), :]
                    face[m, wide_rows(pair), lanes(h)] = cells.astype(BF16)


def unpack_chord(faces, chord_halo):
    p = parity("chord")
    for face, side in zip(faces, (1 - p, p)):
        for group in range(CS // 2):
            both = face[group].astype(F32)
            chord_halo[side, 2 * group] = both[:8]
            chord_halo[side, 2 * group + 1] = both[8:]


def fill_beyond(field, chord_halo, s):
    for side in range(2):
        for m in range(NCONS):
            for h in range(HALVES):
                field[m, s, h, pl.ds(BEYOND[side], 1), :] = chord_halo[side, s, pl.ds(m, 1), lanes(h)]


def pack_chord(edge, faces):
    p = parity("chord")
    for face, side in zip(faces, (1 - p, p)):
        for group in range(CS // 2):
            face[group] = jnp.concatenate([edge[side, 2 * group], edge[side, 2 * group + 1]], axis=0).astype(BF16)


def clear_padding(edge):
    for side in range(2):
        for s in range(CS):
            edge[side, s] = jnp.zeros((8, CN), F32)


def pack_faces(field, edge, faces):
    chord_b, chord_a, span_b, span_a = faces
    pack_chord(edge, (chord_a, chord_b))
    pack_span(field, (span_a, span_b))


START_SPAN = ((NCONS, CC // 2, CN), jnp.int32)
START_CHORD = ((CS // 2, 8, CN), jnp.int32)
START_FACES = [START_CHORD, START_CHORD, START_SPAN, START_SPAN]


def code_pair(high, low, scale):
    code = lambda x: jnp.round(x * scale).astype(jnp.int32)
    return (code(high) << 16) | (code(low) & 0xFFFF)


def decode_pair(word):
    return (word >> 16).astype(F32), ((word << 16) >> 16).astype(F32)


def faces_body(cells, chord_b, chord_a, span_b, span_a, edge):
    clear_padding(edge)
    for s in range(CS):
        for m in range(NCONS):
            edge[0, s, pl.ds(m, 1), :] = cells[m, s, pl.ds(0, 1), :]
            edge[1, s, pl.ds(m, 1), :] = cells[m, s, pl.ds(CC - 1, 1), :]
    p = parity("span")
    for face, side in ((span_a, 1 - p), (span_b, p)):
        for m in range(NCONS):
            for pair in range(CC // 16):
                high, low = (cells[m, side * (CS - 1), rows(2 * pair + i), :] for i in range(2))
                face[m, rows(pair), :] = code_pair(high, low, ADJOINT_CODE)
    p = parity("chord")
    for face, side in ((chord_a, 1 - p), (chord_b, p)):
        for group in range(CS // 2):
            face[group] = code_pair(edge[side, 2 * group], edge[side, 2 * group + 1], ADJOINT_CODE)


def unpack_start(faces, chord_halo, span_halo):
    chord_b, chord_a, span_b, span_a = faces
    p = parity("span")
    for face, side in ((span_a, 1 - p), (span_b, p)):
        for m in range(NCONS):
            for pair in range(CC // 16):
                for i, half in enumerate(decode_pair(face[m, rows(pair), :])):
                    span_halo[side, m, rows(2 * pair + i), :] = half * (1.0 / ADJOINT_CODE)
    p = parity("chord")
    for face, side in ((chord_a, 1 - p), (chord_b, p)):
        for group in range(CS // 2):
            for i, half in enumerate(decode_pair(face[group])):
                chord_halo[side, 2 * group + i] = half * (1.0 / ADJOINT_CODE)


def exchange(faces):
    def swap(face, axis, start):
        count = lax.axis_size(axis)
        pairs = [(i, i + 1) for i in range(start, count - 1, 2)]
        return lax.ppermute(face, axis, pairs + [(b, a) for a, b in pairs])

    chord_b, chord_a, span_b, span_a = faces
    return swap(chord_b, "chord", 1), swap(chord_a, "chord", 0), swap(span_b, "span", 1), swap(span_a, "span", 0)


def normal(centers, h, step, lane_first, lane_last):
    if step > 0:
        source = jnp.where(lane_first, centers[h + 1], centers[h]) if h + 1 < HALVES else centers[h]
        return pltpu.roll(source, LANES - 1, 1)
    source = jnp.where(lane_last, centers[h - 1], centers[h]) if h > 0 else centers[h]
    return pltpu.roll(source, 1, 1)


def stencil(field, span_halo, s, t, edge, factors, energies, bases, coupling, write):
    lane_first, lane_last = mask_of(1, 0), mask_of(1, LANES - 1)
    centers = [[field[m, s, h, chord_rows(t), :] for h in range(HALVES)] for m in range(NCONS)]
    for m in range(NCONS):
        scalars = [coupling[n, m] for n in range(NCONS)]
        for h in range(HALVES):
            spans, (chord_up, chord_low), (normal_up, normal_low) = factors[h]
            mixed = scalars[0] * centers[0][h]
            for n in range(1, NCONS):
                mixed = mixed + scalars[n] * centers[n][h]
            total = bases(m, h, centers[m][h]) + energies[h] * mixed
            for step, side, factor in ((1, 1, spans[0]), (-1, 0, spans[1])):
                if edge != step:
                    total = total + factor * field[m, s + step, h, chord_rows(t), :]
                elif span_halo is not None:
                    total = total + factor * span_halo[side, m, rows(t), lanes(h)]
            total = total + chord_up * field[m, s, h, chord_rows(t, 1), :]
            total = total + chord_low * field[m, s, h, chord_rows(t, -1), :]
            total = total + normal_up * normal(centers[m], h, 1, lane_first, lane_last)
            total = total + normal_low * normal(centers[m], h, -1, lane_first, lane_last)
            write(m, s, t, h, total)


def into_field(out, edge=None):
    def write(m, s, t, h, tile):
        out[m, s, h, chord_rows(t), :] = tile
        if edge is not None and t == 0:
            edge[0, s, pl.ds(m, 1), lanes(h)] = tile[0:1]
        if edge is not None and t == TILES - 1:
            edge[1, s, pl.ds(m, 1), lanes(h)] = tile[7:8]

    return write


def into_rows(out):
    def write(m, s, t, h, tile):
        out[m, s, rows(t), lanes(h)] = tile

    return write


def copy_row(cells, field, s):
    for m in range(NCONS):
        for t in range(TILES):
            for h in range(HALVES):
                field[m, s, h, chord_rows(t), :] = cells[m, s, rows(t), lanes(h)]


def inner_rows(row):
    def inner(s, carry):
        row(s, 0)
        return carry

    lax.fori_loop(1, CS - 1, inner, 0, unroll=7)


def each_row(row):
    row(0, -1)
    inner_rows(row)
    row(CS - 1, 1)


def split_signs(signed, quarter, h):
    pairs = []
    for a in range(3):
        up = jnp.maximum(quarter - signed[a], quarter)
        low = up + signed[a]
        if a == 2 and h == HALVES - 1:
            up = jnp.where(mask_of(1, LANES - 1), 0.0, up)
        if a == 2 and h == 0:
            low = jnp.where(mask_of(1, 0), 0.0, low)
        pairs.append((up, low))
    return pairs


SLOTS = 16


def send_body(pieces, targets, out, taken, words, ordered, target, in_sem, target_sem, out_sem):
    groups = pieces.shape[1] // SLOTS
    take = lambda g: pltpu.make_async_copy(
        pieces.at[:, pl.ds(g * SLOTS, SLOTS)], taken.at[:, pl.ds(g * SLOTS, SLOTS)], in_sem.at[g]
    )
    for g in range(groups):
        take(g).start()
        if g == 0:
            look = pltpu.make_async_copy(targets, target, target_sem)
            look.start()
    look.wait()

    def group(g, carry):
        take(g).wait()
        for c in range(PIECE // LANES):
            read = lambda f: taken[f, pl.ds(pl.multiple_of(g * SLOTS, SLOTS), SLOTS), lanes(c)].astype(F32)
            ratio = 1.0 / read(0)
            codes = [jnp.round((read(1 + a) * ratio - read(5 + a)) * VELOCITY_CODE).astype(jnp.int32) for a in range(3)]
            codes.append(jnp.round(read(4) * ratio * ENERGY_CODE).astype(jnp.int32))
            for w in range(2):
                word = (codes[2 * w] << 16) | (codes[2 * w + 1] & 0xFFFF)
                for part in range(2):
                    at = pl.multiple_of((g * 2 + part) * 64 + c * 8, 8)
                    words[w, pl.ds(at, 8), :] = word[part * 8 : part * 8 + 8]
        for j in range(SLOTS):
            d = target[0, g * SLOTS + j]
            for w in range(2):
                ordered[d, w] = words[w, pl.ds((g * 2 + j // 8) * 64 + j % 8, 8, stride=8), :]
        return carry

    lax.fori_loop(0, groups, group, 0)
    copy = pltpu.make_async_copy(ordered, out, out_sem)
    copy.start()
    copy.wait()


def send_order(pieces, target):
    count = pieces.shape[1]
    return call(
        send_body,
        [((count, 2, 8, LANES), jnp.int32)],
        [pieces, target],
        scratch=[
            pltpu.VMEM(pieces.shape, BF16),
            pltpu.VMEM((2, count * 8, LANES), jnp.int32),
            pltpu.VMEM((count, 2, 8, LANES), jnp.int32),
            pltpu.SMEM(target.shape, jnp.int32),
            pltpu.SemaphoreType.DMA((count // SLOTS,)),
            pltpu.SemaphoreType.DMA,
            pltpu.SemaphoreType.DMA,
        ],
        hbm=(0, 1),
        hbm_outs=(0,),
        cost=3 * MIB,
    )[0]


AHEAD = 6


def right_body(v, state, grad, coupling, out, span_next, chord_next, states, grads, rights, field, in_sem, out_sem):
    copies = lambda s: (
        pltpu.make_async_copy(state.at[:, s], states.at[:, s], in_sem.at[0, s]),
        pltpu.make_async_copy(grad.at[:, s], grads.at[:, s], in_sem.at[1, s]),
    )
    put_out = lambda s: pltpu.make_async_copy(rights.at[:, s], out.at[:, s], out_sem.at[s])
    for s in range(AHEAD):
        for copy in copies(s):
            copy.start()
    row_first, row_last = mask_of(0, 0), mask_of(0, 7)
    copy_row(v, field, 0)

    def row(s, edge):
        if edge < 1:
            copy_row(v, field, s + 1)
        for side in range(2):
            for m in range(NCONS):
                for h in range(HALVES):
                    field[m, s, h, pl.ds(BEYOND[side], 1), :] = jnp.zeros((1, LANES), F32)
        for copy in copies(s):
            copy.wait()
        if edge == 0:

            @pl.when(s + AHEAD - 1 < CS)
            def _():
                for copy in copies(s + AHEAD - 1):
                    copy.start()

        for pair in range(TILES // 2):
            wide = lambda ref, f, h: ref[f, s, wide_rows(pair), lanes(h)].astype(F32)
            fields = [[wide(states, f, h) for h in range(HALVES)] for f in range(NSTATE)]
            gradient = [[wide(grads, m, h) for h in range(HALVES)] for m in range(NCONS)]
            for part in range(2):
                t = pair * 2 + part
                cut = lambda x: x[part * 8 : part * 8 + 8]
                factors, energies, middles = [], [], []
                for h in range(HALVES):
                    ratio = 0.5 / cut(fields[0][h])
                    signed = [cut(fields[1 + a][h]) * ratio - 0.5 * cut(fields[5 + a][h]) for a in range(3)]
                    factors.append(split_signs(signed, 0.125, h))
                    energies.append(-(cut(fields[4][h]) * ratio))
                    middles.append(0.25 - (jnp.abs(signed[0]) + jnp.abs(signed[1]) + jnp.abs(signed[2])))
                    (span_up, span_low), (chord_up, chord_low), _ = factors[h]
                    if edge == -1:
                        span_next[0, rows(t), lanes(h)] = span_low
                    if edge == 1:
                        span_next[1, rows(t), lanes(h)] = span_up
                    if t == 0:
                        chord_next[0, s, :, lanes(h)] = jnp.where(row_first, chord_low, 0.0)
                    if t == TILES - 1:
                        chord_next[1, s, :, lanes(h)] = jnp.where(row_last, chord_up, 0.0)
                base = lambda m, h, center: cut(gradient[m][h]) + middles[h] * center
                stencil(field, None, s, t, edge, factors, energies, base, coupling, into_rows(rights))
        if edge >= 0:
            put_out(s - 1).start()

    each_row(row)
    put_out(CS - 1).start()
    for s in range(CS):
        put_out(s).wait()


def first_body(v, words, owner, right, coupling, span_next, chord_next, fa, fb, fc, fd, out, factor, scaled, ga, gb, gc, gd, placed, rights, field, span_halo, chord_halo, edge_cells, word_sem, right_sem):
    per_row = owner.shape[1] // CS
    take = lambda s: pltpu.make_async_copy(right.at[:, s], rights.at[:, s], right_sem.at[s])
    landed = lambda s: placed.at[:, pl.ds(pl.multiple_of(s * per_row * 8, 8), per_row * 8)]
    whole = lambda s: pltpu.make_async_copy(landed(s), landed(s), word_sem.at[s])

    def gather(s, carry):
        for j in range(per_row):
            k = s * per_row + j
            pltpu.make_async_copy(
                words.at[owner[0, k]], placed.at[:, pl.ds(pl.multiple_of(k * 8, 8), 8)], word_sem.at[s]
            ).start()
        take(s).start()
        return carry

    lax.fori_loop(0, CS, gather, 0)
    unpack_start((fa, fb, fc, fd), chord_halo, span_halo)
    clear_padding(edge_cells)
    copy_row(v, field, 0)

    def row(s, edge):
        if edge < 1:
            copy_row(v, field, s + 1)
        fill_beyond(field, chord_halo, s)
        whole(s).wait()
        take(s).wait()
        for t in range(TILES):
            factors, energies, scales = [], [], []
            for h in range(HALVES):
                pair = [placed[w, pl.ds((s * 8 + t * 2) * 8 + h, 8, stride=2), :] for w in range(2)]
                codes = [*decode_pair(pair[0]), *decode_pair(pair[1])]
                size = jnp.abs(codes[0]) + jnp.abs(codes[1]) + jnp.abs(codes[2])
                scale = 1.0 / (1.75 + (0.5 / VELOCITY_CODE) * size)
                signed = [codes[a] * ((0.5 / VELOCITY_CODE) * scale) for a in range(3)]
                pairs = split_signs(signed, 0.125 * scale, h)
                energy = codes[3] * ((-0.5 / ENERGY_CODE) * scale)
                factors.append(pairs)
                energies.append(energy)
                scales.append(scale)
                for a in range(3):
                    factor[2 * a, s, rows(t), lanes(h)] = pairs[a][0]
                    factor[2 * a + 1, s, rows(t), lanes(h)] = pairs[a][1]
                factor[6, s, rows(t), lanes(h)] = energy

            def base(m, h, center):
                value = rights[m, s, rows(t), lanes(h)]
                if edge != 0:
                    side = 0 if edge == -1 else 1
                    value = value + span_next[side, rows(t), lanes(h)] * span_halo[side, m, rows(t), lanes(h)]
                if t == 0:
                    value = value + chord_next[0, s, :, lanes(h)] * field[m, s, h, chord_rows(t, -1), :]
                if t == TILES - 1:
                    value = value + chord_next[1, s, :, lanes(h)] * field[m, s, h, chord_rows(t, 1), :]
                value = value * scales[h]
                scaled[m, s, rows(t), lanes(h)] = value
                return value

            stencil(field, span_halo, s, t, edge, factors, energies, base, coupling, into_field(out, edge_cells))

    each_row(row)
    pack_faces(out, edge_cells, (ga, gb, gc, gd))


def sweep_row(field, span_halo, factor, scaled, coupling, out, edge_cells, s, edge):
    for t in range(TILES):
        read = lambda i, h: factor[i, s, rows(t), lanes(h)]
        factors = [[(read(2 * a, h), read(2 * a + 1, h)) for a in range(3)] for h in range(HALVES)]
        energies = [read(6, h) for h in range(HALVES)]
        base = lambda m, h, center: scaled[m, s, rows(t), lanes(h)]
        stencil(field, span_halo, s, t, edge, factors, energies, base, coupling, into_field(out, edge_cells))


def inner_body(before, factor, scaled, coupling, fc, fd, field, out, edge_cells, chord_halo):
    unpack_chord((fc, fd), chord_halo)
    clear_padding(edge_cells)
    for s in (0, CS - 1):
        fill_beyond(field, chord_halo, s)

    def row(s, edge):
        fill_beyond(field, chord_halo, s)
        sweep_row(field, None, factor, scaled, coupling, out, edge_cells, s, edge)

    inner_rows(row)


def ends_body(field, factor, scaled, coupling, fa, fb, before, before_edge, out, edge_cells, ga, gb, gc, gd, span_halo):
    unpack_span((fa, fb), span_halo)
    for s, edge in ((0, -1), (CS - 1, 1)):
        sweep_row(field, span_halo, factor, scaled, coupling, out, edge_cells, s, edge)
    pack_faces(out, edge_cells, (ga, gb, gc, gd))


def row_copies(cells, out, sem, s):
    return [
        pltpu.make_async_copy(cells.at[:, s, h, pl.ds(HOME, CC), :], out.at[:, s, :, lanes(h)], sem.at[h, s])
        for h in range(HALVES)
    ]


SPLIT = 10


def last_inner_body(before, factor, scaled, coupling, fc, fd, field, out, cells, chord_halo, out_sem):
    unpack_chord((fc, fd), chord_halo)
    for s in (0, CS - 1):
        fill_beyond(field, chord_halo, s)

    def row(s, edge):
        fill_beyond(field, chord_halo, s)
        sweep_row(field, None, factor, scaled, coupling, cells, None, s, edge)

        @pl.when((s > 1) & (s <= SPLIT))
        def _():
            for copy in row_copies(cells, out, out_sem, s - 1):
                copy.start()

    inner_rows(row)
    for s in range(1, SPLIT):
        for copy in row_copies(cells, out, out_sem, s):
            copy.wait()


def last_ends_body(field, factor, scaled, coupling, fa, fb, before, cells, out, ends, span_halo, out_sem):
    for s in range(SPLIT, CS - 1):
        for copy in row_copies(cells, out, out_sem, s):
            copy.start()
    unpack_span((fa, fb), span_halo)
    for s, edge in ((0, -1), (CS - 1, 1)):
        sweep_row(field, span_halo, factor, scaled, coupling, ends, None, s, edge)
        for copy in row_copies(ends, out, out_sem, s):
            copy.start()
    for s in range(SPLIT, CS - 1):
        for copy in row_copies(cells, out, out_sem, s):
            copy.wait()
    for s in (0, CS - 1):
        for copy in row_copies(ends, out, out_sem, s):
            copy.wait()


BLOCK = (NCONS, CS, CC, CN)
CELLS = (BLOCK, F32)
ROW_SEMS = pltpu.SemaphoreType.DMA((CS,))


def shards(adjoint_next, objective_grad, state_next, checkpoint_pieces, slot_target, piece_owner, coupling):
    outgoing = send_order(checkpoint_pieces, slot_target)
    incoming = lax.all_to_all(outgoing, ("span", "chord"), split_axis=0, concat_axis=0, tiled=True)
    halo = exchange(call(faces_body, START_FACES, [adjoint_next], scratch=[CHORD_HALO], cost=MIB // 2))
    right, span_next, chord_next = call(
        right_body,
        [CELLS, ((2, CC, CN), F32), ((2, CS, 8, CN), F32)],
        [adjoint_next, state_next, objective_grad, coupling],
        scratch=[
            pltpu.VMEM((NSTATE, CS, CC, CN), BF16),
            pltpu.VMEM(BLOCK, BF16),
            pltpu.VMEM(BLOCK, F32),
            FIELD_SCRATCH,
            pltpu.SemaphoreType.DMA((2, CS)),
            ROW_SEMS,
        ],
        smem=(3,),
        hbm=(1, 2),
        hbm_outs=(0,),
        cost=9 * MIB,
    )
    adjoint, factor, scaled, *faces = call(
        first_body,
        [FIELD, ((7, CS, CC, CN), F32), CELLS, *FACES],
        [adjoint_next, incoming, piece_owner, right, coupling, span_next, chord_next, *halo],
        scratch=[
            pltpu.VMEM((2, piece_owner.shape[1] * 8, LANES), jnp.int32),
            pltpu.VMEM(BLOCK, F32),
            FIELD_SCRATCH,
            SPAN_HALO,
            CHORD_HALO,
            CHORD_HALO,
            ROW_SEMS,
            ROW_SEMS,
        ],
        smem=(2, 4),
        hbm=(1, 3),
        cost=9 * MIB,
    )
    for sweep in range(2, SWEEPS + 1):
        chord_b, chord_a, span_b, span_a = exchange(faces)
        fixed = [factor, scaled, coupling]
        if sweep == SWEEPS:
            adjoint, *inner = call(
                last_inner_body,
                [FIELD, CELLS, FIELD],
                [adjoint, *fixed, chord_a, chord_b],
                scratch=[CHORD_HALO, pltpu.SemaphoreType.DMA((HALVES, CS))],
                smem=(3,),
                hbm_outs=(1,),
                aliases={0: 0},
                cost=8 * MIB,
            )
            return call(
                last_ends_body,
                [CELLS],
                [adjoint, *fixed, span_a, span_b, *inner],
                scratch=[FIELD_SCRATCH, SPAN_HALO, pltpu.SemaphoreType.DMA((HALVES, CS))],
                smem=(3,),
                hbm=(6,),
                hbm_outs=(0,),
                aliases={6: 0},
                cost=MIB,
            )[0]
        adjoint, *inner = call(
            inner_body,
            [FIELD, FIELD, EDGES],
            [adjoint, *fixed, chord_a, chord_b],
            scratch=[CHORD_HALO],
            smem=(3,),
            aliases={0: 0},
            cost=8 * MIB,
        )
        adjoint, _, *faces = call(
            ends_body,
            [FIELD, EDGES, *FACES],
            [adjoint, *fixed, span_a, span_b, *inner],
            scratch=[SPAN_HALO],
            smem=(3,),
            aliases={6: 0, 7: 1},
            cost=MIB,
        )


def solution(mesh):
    placed = (
        P(None, "span", "chord", None),
        P(None, "span", "chord", None),
        P(None, "span", "chord", None),
        P(None, ("span", "chord"), None),
        P(("span", "chord"), None),
        P(("span", "chord"), None),
        P(),
    )
    return jax.shard_map(
        shards,
        mesh=mesh,
        in_specs=placed,
        out_specs=P(None, "span", "chord", None),
        check_vma=False,
    )
```
